128 devices in a mesh: ka: 16 (over z, y), row: 8 (over x, core).
Axes of the slice: x: 4, y: 4, z: 4, core: 2. Of those that a mesh axis runs over, the one named last changes fastest.
Arguments:
- packet: float32 [32, 384, 128, 128], P('ka', None, 'row'), may hold values from -6 to 6
- previous: float32 [32, 384, 128, 128], P('ka', None, 'row'), may hold values from -6 to 6
- basis_sizes: int32 [32], P('ka'), may hold values from 96 to 384, as said below
- centrifugal: float32 [32, 384], P('ka'), may hold values from 0.1 to 2
- coriolis: float32 [32, 384], replicated, may hold values from -3 to 3
- inertia: float32 [128, 128], replicated, may hold values from 0.25 to 4
- damping: float32 [128], P('row'), may hold values from 0.6 to 1
- radial_kin: float32 [128, 128], replicated, may hold values from -0.5 to 0.5
- stretch_kin: float32 [128, 128], replicated, may hold values from -0.5 to 0.5
- legendre: float32 [32, 512, 384], P('ka'), may hold values from -0.3125 to 0.3125
- potential: float32 [512, 128, 128], P(None, 'row'), may hold values from -1 to 1
Outputs:
- advanced: float32 [32, 384, 128, 128], P('ka', None, 'row')
The draws below stay inside these ranges and needn't reach their ends.
Inputs may be any that keep to these rules, and one draw needn't show every extreme that they name: `basis_sizes`: one helicity block has exactly 384 live basis functions and another exactly 96.
All inputs are finite; a program needn't handle non-finite values.
Results may differ from the reference program's by a relative error of at most 0.0003.
Values sent between devices are 32-bit elements; how exact they have to be, the bound alone decides.
No kernel may reach another device: no remote copies, remote signals or barrier semaphores. Data moves between devices by JAX's collectives and lax.ppermute only.
A program may use at most 192 MiB of HBM per device.

```python
import math
import jax
import jax.numpy as jnp
from jax import lax

JMAX = 384
NANG = 512
NR = 128
NRR = 128
NK = 32


def draw_basis_sizes(key, part):
    block_sizes = jax.random.randint(jax.random.fold_in(key, 11), (NK,), JMAX // 4, JMAX + 1)
    shuffled = jax.random.permutation(jax.random.fold_in(key, 17), NK)
    block_sizes = block_sizes.at[shuffled[0]].set(JMAX)
    block_sizes = block_sizes.at[shuffled[1]].set(JMAX // 4)
    return block_sizes.astype(jnp.int32)


def level_of(rng, dims, split, low, largest):
    loudness = 1.0
    for dim, shards_of in split:
        draws = jax.random.uniform(jax.random.fold_in(jax.random.fold_in(rng, 6), dim), (shards_of,), jnp.float32, low / len(split), largest / len(split))
        loudness = loudness * jnp.repeat(jnp.exp(draws), dims[dim] // shards_of).reshape((-1,) + (1,) * (len(dims) - 1 - dim))
    return loudness


def bell_draw(rng, dims, spread, bound, cuts=(), held_as=jnp.bfloat16):
    values = spread * jax.random.normal(rng, dims, jnp.float32)
    if cuts:
        values = values * level_of(rng, dims, cuts, -0.22, 0.18)
    return jnp.clip(values, -bound, bound).astype(held_as)


def setup_inputs(seed: int = 0) -> dict:
    streams_of = jax.random.split(jax.random.key(seed), 12)
    packet = bell_draw(streams_of[0], (NK, JMAX, NR, NRR), 1.0, 6.0, ((0, 16), (2, 8)), jnp.float32)
    previous = bell_draw(streams_of[1], (NK, JMAX, NR, NRR), 1.0, 6.0, ((0, 16), (2, 8)), jnp.float32)
    basis_sizes = draw_basis_sizes(jax.random.fold_in(streams_of[11], 71), 0)
    centrifugal = jnp.clip(jnp.exp(math.log(2.0) - 2.9957323 * jax.random.uniform(streams_of[3], (NK, JMAX), jnp.float32) ** level_of(streams_of[3], (NK, JMAX), ((0, 16),), -0.2, 0.2)), 0.1, 2.0)
    coriolis = bell_draw(streams_of[4], (NK, JMAX), 0.5, 3.0, (), jnp.float32)
    inertia = jnp.clip(jnp.exp(jax.random.uniform(streams_of[5], (NR, NRR), jnp.float32, math.log(0.25), math.log(4.0))), 0.25, 4.0)
    damping = jnp.clip(0.6 + 0.39999998 * jax.random.uniform(streams_of[6], (NR,), jnp.float32) ** level_of(streams_of[6], (NR,), ((0, 8),), -0.2, 0.2), 0.6, 1.0)
    radial_kin = bell_draw(streams_of[7], (NR, NR), NR ** -0.5, 0.5, (), jnp.float32)
    stretch_kin = bell_draw(streams_of[8], (NRR, NRR), NRR ** -0.5, 0.5, (), jnp.float32)
    legendre = bell_draw(streams_of[9], (NK, NANG, JMAX), JMAX ** -0.5, 0.3125, ((0, 16),), jnp.float32)
    potential = jnp.clip(jax.random.uniform(streams_of[10], (NANG, NR, NRR), jnp.float32, -1.0, 1.0) * level_of(streams_of[10], (NANG, NR, NRR), ((1, 8),), -0.4, 0.0), -1.0, 1.0)
    return {"packet": packet, "previous": previous, "basis_sizes": basis_sizes, "centrifugal": centrifugal, "coriolis": coriolis, "inertia": inertia, "damping": damping, "radial_kin": radial_kin, "stretch_kin": stretch_kin, "legendre": legendre, "potential": potential}


def reference(packet, previous, basis_sizes, centrifugal, coriolis, inertia, damping, radial_kin, stretch_kin, legendre, potential):
    precise = lax.Precision.HIGHEST
    basis_index = jnp.arange(JMAX, dtype=jnp.int32)
    live_mask = (basis_index[None, :] < basis_sizes[:, None]).astype(jnp.float32)

    def fetch(position):
        clipped = jnp.clip(position, 0, NK - 1).astype(jnp.int32)
        in_range = ((position >= 0) & (position < NK)).astype(jnp.float32)
        block = lax.dynamic_index_in_dim(packet, clipped, 0, keepdims=False)
        row_mask = lax.dynamic_index_in_dim(live_mask, clipped, 0, keepdims=False)
        return block * row_mask[:, None, None] * in_range

    def one_block(block_id):
        masked = fetch(block_id)
        upper_block = fetch(block_id + 1)
        lower_block = fetch(block_id - 1)
        coupling_here = lax.dynamic_index_in_dim(coriolis, block_id, 0, keepdims=False)
        coupling_before = lax.dynamic_index_in_dim(coriolis, jnp.maximum(block_id - 1, 0).astype(jnp.int32), 0, keepdims=False)
        radial_term = jnp.einsum('rs,jsx->jrx', radial_kin, masked, precision=precise) + jnp.einsum('jrz,xz->jrx', masked, stretch_kin, precision=precise)
        rotation_term = lax.dynamic_index_in_dim(centrifugal, block_id, 0, keepdims=False)[:, None, None] * inertia[None] * masked
        angular = lax.dynamic_index_in_dim(legendre, block_id, 0, keepdims=False)
        on_grid = jnp.einsum('gj,jy->gy', angular, masked.reshape(JMAX, NR * NRR), precision=precise) * potential.reshape(NANG, NR * NRR)
        potential_term = jnp.einsum('gj,gy->jy', angular, on_grid, precision=precise).reshape(JMAX, NR, NRR)
        coupling_term = inertia[None] * (coupling_here[:, None, None] * upper_block + coupling_before[:, None, None] * lower_block)
        hamilton = radial_term + rotation_term + potential_term + coupling_term
        earlier = lax.dynamic_index_in_dim(previous, block_id, 0, keepdims=False)
        row_mask = lax.dynamic_index_in_dim(live_mask, block_id, 0, keepdims=False)
        factor = damping[None, :, None]
        return row_mask[:, None, None] * factor * (2.0 * hamilton - factor * earlier)

    return lax.map(one_block, jnp.arange(NK, dtype=jnp.int32))
```

```python
import functools

import jax
import jax.numpy as jnp
from jax import lax
from jax.experimental import pallas as pl
from jax.experimental.pallas import tpu as pltpu
from jax.sharding import PartitionSpec as P

F32 = jnp.float32
BF16 = jnp.bfloat16
MIB = 1 << 20


def from_behind(x, axis, by):
    peers = lax.axis_size(axis)
    pairs = [(i, i + by) for i in range(peers) if 0 <= i + by < peers]
    return lax.ppermute(x, axis, pairs)


def exchange(x):
    return lax.all_to_all(x, "row", split_axis=0, concat_axis=0, tiled=True)


def halves(x):
    high = x.astype(BF16)
    return high, (x - high.astype(F32)).astype(BF16)


def halves_outside(x):
    high = lax.reduce_precision(x, 8, 7)
    return high.astype(BF16), (x - high).astype(BF16)


def local_kernel(
    sizes, centrifugal, x_ref, previous_ref, potential_ref, legendre_ref, stretch_ref,
    inertia_ref, factor_ref, out_ref, acc, ahead, back,
):
    block = pl.program_id(0)
    live = sizes[block]
    angles, basis = legendre_ref.shape[1:]
    radial = inertia_ref.shape[0]
    rows = basis * radial
    high, low = halves(legendre_ref[0])
    ahead[:, :basis] = high
    ahead[:, basis : 2 * basis] = high
    ahead[:, 2 * basis :] = low
    high, low = halves(legendre_ref[0].T)
    back[:, :angles] = high
    back[:, angles : 2 * angles] = high
    back[:, 2 * angles :] = low

    piece = rows // 8

    @pl.loop(0, 8)
    def _(i):
        at = pl.ds(pl.multiple_of(i * piece, piece), piece)
        high, low = halves(x_ref[0, at, :])
        both = jnp.dot(
            jnp.concatenate([high, low], 1), stretch_ref[...], preferred_element_type=F32
        )
        acc[at, :] = both[:, :128] + both[:, 128:]

    mask = lax.broadcasted_iota(jnp.int32, (basis, 256), 0) < live

    @pl.loop(0, radial // 2)
    def _(i):
        r = 2 * i
        here = [pl.ds(r + k, basis, stride=radial) for k in range(2)]
        there = [pl.ds(r + k, angles, stride=radial) for k in range(2)]
        m = jnp.concatenate([x_ref[0, at, :] for at in here], 1)
        m = jnp.where(mask, m, 0.0)
        high, low = halves(m)
        grid = jnp.dot(
            ahead[...], jnp.concatenate([high, low, high], 0), preferred_element_type=F32
        )
        grid = grid * jnp.concatenate([potential_ref[at, :] for at in there], 1)
        high, low = halves(grid)
        term = jnp.dot(
            back[...], jnp.concatenate([high, low, high], 0), preferred_element_type=F32
        )
        for k in range(2):
            acc[here[k], :] += term[:, 128 * k : 128 * (k + 1)]

    inertia = inertia_ref[...]
    factor = factor_ref[...]

    @pl.loop(0, basis // 8)
    def _(i):
        for k in range(8):
            j = i * 8 + k
            at = pl.ds(pl.multiple_of(j * radial, radial), radial)
            value = acc[at, :] + (centrifugal[block, j] * inertia) * x_ref[0, at, :]
            value = factor * (2.0 * value - factor * previous_ref[0, at, :])
            out_ref[0, at, :] = jnp.where(j < live, value, 0.0)


def local_terms(sizes, centrifugal, x, previous, potential, legendre, stretch, inertia, factor):
    blocks, angles, basis = legendre.shape
    rows = x.shape[1]
    whole = pl.BlockSpec((1, rows, 128), lambda k: (k, 0, 0))
    smem = pl.BlockSpec(memory_space=pltpu.SMEM)
    once = lambda shape: pl.BlockSpec(shape, lambda k: (0,) * len(shape))
    return pl.pallas_call(
        local_kernel,
        grid=(blocks,),
        in_specs=[
            smem, smem, whole, whole, once(potential.shape),
            pl.BlockSpec((1, angles, basis), lambda k: (k, 0, 0)),
            once(stretch.shape), once(inertia.shape), once(factor.shape),
        ],
        out_specs=whole,
        out_shape=jax.ShapeDtypeStruct(x.shape, F32),
        scratch_shapes=[
            pltpu.VMEM((rows, 128), F32),
            pltpu.VMEM((angles, 3 * basis), BF16),
            pltpu.VMEM((basis, 3 * angles), BF16),
        ],
        compiler_params=pltpu.CompilerParams(vmem_limit_bytes=52 * MIB),
        cost_estimate=pl.CostEstimate(
            flops=12_000_000_000, bytes_accessed=27_000_000, transcendentals=0
        ),
        name="local_terms",
    )(sizes, centrifugal, x, previous, potential, legendre, stretch, inertia, factor)


def radial_kernel(matrix_ref, x_ref, out_ref):
    peers, columns, rows, width = x_ref.shape
    for c in range(0, columns, 2):
        m = jnp.concatenate(
            [x_ref[:, c + k].reshape(peers * rows, width) for k in range(2)], 1
        )
        high, low = halves(m)
        both = jnp.dot(
            matrix_ref[...], jnp.concatenate([high, low], 0), preferred_element_type=F32
        )
        total = both[:128] + both[128:]
        for k in range(2):
            out_ref[:, c + k] = total[:, 128 * k : 128 * (k + 1)].reshape(peers, rows, width)


def radial_apply(matrix, received):
    peers, columns, rows, width = received.shape
    some = pl.BlockSpec((peers, 8, rows, width), lambda i: (0, i, 0, 0))
    return pl.pallas_call(
        radial_kernel,
        grid=(columns // 8,),
        in_specs=[pl.BlockSpec(matrix.shape, lambda i: (0, 0)), some],
        out_specs=some,
        out_shape=jax.ShapeDtypeStruct(received.shape, F32),
        cost_estimate=pl.CostEstimate(
            flops=columns * 20_000_000, bytes_accessed=2 * 4 * received.size, transcendentals=0
        ),
        name="radial_apply",
    )(matrix, received)


def middle_kernel(
    sizes, coriolis, out_in, x_ref, lower_ref, upper_ref, first_ref, inertia_ref, factor_ref, out_ref
):
    step = pl.program_id(0)
    radial = inertia_ref.shape[0]
    count = x_ref.shape[1] // radial
    inertia = inertia_ref[...]
    double = 2.0 * factor_ref[...]
    both = double * inertia
    below, above = sizes[0], sizes[1]

    @pl.loop(0, count // 4)
    def _(i):
        for k in range(4):
            local = i * 4 + k
            j = step * count + local
            at = pl.ds(pl.multiple_of(local * radial, radial), radial)
            here = jnp.where(j < below, x_ref[0, at, :], 0.0)
            there = jnp.where(j < above, x_ref[1, at, :], 0.0)
            low = coriolis[1, j] * there + coriolis[0, j] * lower_ref[at, :]
            high = coriolis[2, j] * upper_ref[at, :] + coriolis[1, j] * here
            out_ref[0, at, :] = out_in[0, at, :] + jnp.where(j < below, both * low, 0.0)
            out_ref[1, at, :] = out_in[1, at, :] + jnp.where(j < above, both * high, 0.0)

    @pl.when(step == 0)
    def _():
        @pl.loop(0, count // 4)
        def _(i):
            for k in range(4):
                j = i * 4 + k
                at = pl.ds(pl.multiple_of(j * radial, radial), radial)
                for b in range(2):
                    out_ref[b, at, :] += jnp.where(j < sizes[b], double * first_ref[b, at, :], 0.0)


def middle_terms(sizes, coriolis, out, x, lower, upper, first, inertia, factor):
    blocks, rows, width = x.shape
    parts = 4
    smem = pl.BlockSpec(memory_space=pltpu.SMEM)
    pair = pl.BlockSpec((blocks, rows // parts, width), lambda i: (0, i, 0))
    one = pl.BlockSpec((rows // parts, width), lambda i: (i, 0))
    small = pl.BlockSpec(inertia.shape, lambda i: (0, 0))
    return pl.pallas_call(
        middle_kernel,
        grid=(parts,),
        in_specs=[
            smem, smem, pair, pair, one, one,
            pl.BlockSpec(first.shape, lambda i: (0, 0, 0)), small, small,
        ],
        out_specs=pair,
        out_shape=jax.ShapeDtypeStruct(out.shape, F32),
        input_output_aliases={2: 0},
        compiler_params=pltpu.CompilerParams(vmem_limit_bytes=40 * MIB),
        cost_estimate=pl.CostEstimate(flops=30_000_000, bytes_accessed=27_000_000, transcendentals=0),
        name="middle_terms",
    )(sizes, coriolis, out, x, lower, upper, first, inertia, factor)


def add_second_kernel(sizes, out_in, back_ref, factor_ref, out_ref):
    radial = factor_ref.shape[0]
    basis = out_in.shape[0] // (2 * radial)
    first = basis // 4
    kept = back_ref.shape[0] // radial
    double = 2.0 * factor_ref[...]
    below, above = sizes[0], sizes[1]
    taken = below - first
    out_ref[...] = out_in[...]

    def add(target, source):
        at = pl.ds(pl.multiple_of(target * radial, radial), radial)
        of = pl.ds(pl.multiple_of(source * radial, radial), radial)
        out_ref[at, :] += double * back_ref[of, :]

    @pl.loop(0, taken)
    def _(i):
        add(first + i, i)

    @pl.loop(0, jnp.minimum(above - first, kept - taken))
    def _(i):
        add(basis + first + i, taken + i)


def add_second(sizes, out, back, factor):
    smem = pl.BlockSpec(memory_space=pltpu.SMEM)
    full = lambda a: pl.BlockSpec(a.shape, lambda: (0, 0))
    return pl.pallas_call(
        add_second_kernel,
        in_specs=[smem, full(out), full(back), full(factor)],
        out_specs=full(out),
        out_shape=jax.ShapeDtypeStruct(out.shape, F32),
        input_output_aliases={1: 0},
        compiler_params=pltpu.CompilerParams(vmem_limit_bytes=40 * MIB),
        cost_estimate=pl.CostEstimate(flops=3_000_000, bytes_accessed=15_000_000, transcendentals=0),
        name="add_second",
    )(sizes, out, back, factor)


def add_tail_kernel(sizes, skipped, out_in, back_ref, factor_ref, out_ref):
    radial = factor_ref.shape[0]
    double = 2.0 * factor_ref[...]
    out_ref[...] = out_in[...]

    @pl.loop(0, skipped[1])
    def _(i):
        at = pl.ds(pl.multiple_of((skipped[0] + i) * radial, radial), radial)
        of = pl.ds(pl.multiple_of(i * radial, radial), radial)
        out_ref[at, :] += double * back_ref[of, :]


def add_tail(sizes, skipped, out, back, factor):
    smem = pl.BlockSpec(memory_space=pltpu.SMEM)
    last = pl.BlockSpec(back.shape, lambda i: (out.shape[0] // back.shape[0] - 1, 0))
    full = lambda a: pl.BlockSpec(a.shape, lambda i: (0, 0))
    return pl.pallas_call(
        add_tail_kernel,
        grid=(1,),
        in_specs=[smem, smem, last, full(back), full(factor)],
        out_specs=last,
        out_shape=jax.ShapeDtypeStruct(out.shape, F32),
        input_output_aliases={2: 0},
        compiler_params=pltpu.CompilerParams(vmem_limit_bytes=30 * MIB),
        cost_estimate=pl.CostEstimate(flops=1_000_000, bytes_accessed=6_300_000, transcendentals=0),
        name="add_tail",
    )(sizes, skipped, out, back, factor)


def shards(
    packet, previous, basis_sizes, centrifugal, coriolis, inertia, damping,
    radial_kin, stretch_kin, legendre, potential,
):
    blocks, basis, radial, width = packet.shape
    peers = lax.axis_size("row")
    ka = lax.axis_index("ka")
    row = lax.axis_index("row")
    columns = blocks * basis
    first = basis // 4
    kept = 5 * columns // 12
    tail = columns - 2 * first - kept
    unit = tail // 4

    flat = packet.reshape(columns, radial, width)
    chunk_a = jnp.concatenate([flat[:first], flat[basis : basis + first]], 0)
    got_a = exchange(chunk_a)
    rest = jnp.concatenate([flat[first:basis], flat[basis + first :]], 0)
    rest = lax.dynamic_update_slice(rest, flat[basis + first :], (basis_sizes[0] - first, 0, 0))
    got_b = exchange(rest[:kept])

    live_mask = (lax.broadcasted_iota(jnp.int32, (blocks, basis), 1) < basis_sizes[:, None]).astype(F32)
    masked = packet * live_mask[:, :, None, None]
    upper = from_behind(masked[:1], "ka", -1).reshape(basis * radial, width)
    lower = from_behind(masked[1:], "ka", 1).reshape(basis * radial, width)

    inertia_local = lax.dynamic_slice_in_dim(inertia, row * radial, radial, 0)
    factor = jnp.broadcast_to(damping[:, None], (radial, width))
    t_high, t_low = halves_outside(radial_kin)
    t_high, t_low = [jnp.concatenate([t, t], 1) for t in (t_high, t_low)]
    matrix = jnp.concatenate([t_high, t_low], 0)
    s_high, s_low = halves_outside(stretch_kin.T)
    stretch = jnp.concatenate([jnp.concatenate([s_high, s_low], 1)] * 2, 0)
    start = jnp.maximum(ka * blocks - 1, 0)
    coupling = jnp.concatenate(
        [lax.dynamic_slice_in_dim(coriolis, start, 1, 0),
         lax.dynamic_slice_in_dim(coriolis, ka * blocks, blocks, 0)], 0
    )

    rows = basis * radial
    out = local_terms(
        basis_sizes, centrifugal, packet.reshape(blocks, rows, width),
        previous.reshape(blocks, rows, width),
        potential.reshape(potential.shape[0] * radial, width),
        legendre, stretch, inertia_local, factor,
    )

    def apply(got):
        shape = got.shape
        made = radial_apply(matrix, got.reshape(peers, shape[0] // peers, radial, width))
        return made.reshape(shape)

    back_a = exchange(apply(got_a))
    back_b = exchange(apply(got_b))
    live = basis_sizes[0] + basis_sizes[1]
    over = jnp.maximum(live - 2 * first - kept, 0)

    def take(n):
        def run(rest):
            if n == 0:
                return jnp.zeros((tail, radial, width), F32)
            done = exchange(apply(exchange(rest[kept : kept + n * unit])))
            return jnp.pad(done, ((0, tail - n * unit), (0, 0), (0, 0)))
        return run

    back_t = lax.switch((over + unit - 1) // unit, [take(n) for n in range(5)], rest)

    out = middle_terms(
        basis_sizes, coupling, out, packet.reshape(blocks, rows, width), lower, upper,
        back_a.reshape(blocks, first * radial, width), inertia_local, factor,
    )
    out = add_second(
        basis_sizes, out.reshape(columns * radial, width), back_b.reshape(kept * radial, width), factor
    )
    begin = kept + 2 * first - basis_sizes[0] - (basis - tail)
    out = add_tail(
        basis_sizes, jnp.stack([begin, over]).astype(jnp.int32), out,
        back_t.reshape(tail * radial, width), factor,
    )
    return out.reshape(packet.shape)


def solution(mesh):
    in_specs = (
        P("ka", None, "row", None),
        P("ka", None, "row", None),
        P("ka"),
        P("ka", None),
        P(),
        P(),
        P("row"),
        P(),
        P(),
        P("ka", None, None),
        P(None, "row", None),
    )
    out_specs = P("ka", None, "row", None)
    return jax.shard_map(shards, mesh=mesh, in_specs=in_specs, out_specs=out_specs, check_vma=False)
```

```python
import functools

import jax
import jax.numpy as jnp
from jax import lax
from jax.experimental import pallas as pl
from jax.experimental.pallas import tpu as pltpu
from jax.sharding import PartitionSpec as P

F32 = jnp.float32
BF16 = jnp.bfloat16
MIB = 1 << 20


def from_behind(x, axis, by):
    peers = lax.axis_size(axis)
    pairs = [(i, i + by) for i in range(peers) if 0 <= i + by < peers]
    return lax.ppermute(x, axis, pairs)


def exchange(x):
    return lax.all_to_all(x, "row", split_axis=0, concat_axis=0, tiled=True)


def halves(x):
    high = x.astype(BF16)
    return high, (x - high.astype(F32)).astype(BF16)


def halves_outside(x):
    high = lax.reduce_precision(x, 8, 7)
    return high.astype(BF16), (x - high).astype(BF16)


def local_kernel(
    block, sizes, centrifugal, x_ref, previous_ref, potential_ref, legendre_ref, stretch_ref,
    inertia_ref, factor_ref, out_ref, acc, ahead, back,
):
    live = sizes[block]
    angles, basis = legendre_ref.shape[1:]
    radial = inertia_ref.shape[0]
    rows = basis * radial
    high, low = halves(legendre_ref[0])
    ahead[:, :basis] = high
    ahead[:, basis : 2 * basis] = high
    ahead[:, 2 * basis :] = low
    high, low = halves(legendre_ref[0].T)
    back[:, :angles] = high
    back[:, angles : 2 * angles] = high
    back[:, 2 * angles :] = low

    piece = rows // 8

    @pl.loop(0, 8)
    def _(i):
        at = pl.ds(pl.multiple_of(i * piece, piece), piece)
        high, low = halves(x_ref[0, at, :])
        both = jnp.dot(
            jnp.concatenate([high, low], 1), stretch_ref[...], preferred_element_type=F32
        )
        acc[at, :] = both[:, :128] + both[:, 128:]

    mask = lax.broadcasted_iota(jnp.int32, (basis, 256), 0) < live

    @pl.loop(0, radial // 2)
    def _(i):
        r = 2 * i
        here = [pl.ds(r + k, basis, stride=radial) for k in range(2)]
        there = [pl.ds(r + k, angles, stride=radial) for k in range(2)]
        m = jnp.concatenate([x_ref[0, at, :] for at in here], 1)
        m = jnp.where(mask, m, 0.0)
        high, low = halves(m)
        grid = jnp.dot(
            ahead[...], jnp.concatenate([high, low, high], 0), preferred_element_type=F32
        )
        grid = grid * jnp.concatenate([potential_ref[at, :] for at in there], 1)
        high, low = halves(grid)
        term = jnp.dot(
            back[...], jnp.concatenate([high, low, high], 0), preferred_element_type=F32
        )
        for k in range(2):
            acc[here[k], :] += term[:, 128 * k : 128 * (k + 1)]

    inertia = inertia_ref[...]
    factor = factor_ref[...]

    @pl.loop(0, basis // 8)
    def _(i):
        for k in range(8):
            j = i * 8 + k
            at = pl.ds(pl.multiple_of(j * radial, radial), radial)
            value = acc[at, :] + (centrifugal[block, j] * inertia) * x_ref[0, at, :]
            value = factor * (2.0 * value - factor * previous_ref[0, at, :])
            out_ref[0, at, :] = jnp.where(j < live, value, 0.0)


def local_terms(block, sizes, centrifugal, x, previous, potential, legendre, stretch, inertia, factor):
    angles, basis = legendre.shape[1:]
    rows = x.shape[1]
    whole = pl.BlockSpec((1, rows, 128), lambda k: (block, 0, 0))
    smem = pl.BlockSpec(memory_space=pltpu.SMEM)
    once = lambda shape: pl.BlockSpec(shape, lambda k: (0,) * len(shape))
    return pl.pallas_call(
        functools.partial(local_kernel, block),
        grid=(1,),
        in_specs=[
            smem, smem, whole, whole, once(potential.shape),
            pl.BlockSpec((1, angles, basis), lambda k: (block, 0, 0)),
            once(stretch.shape), once(inertia.shape), once(factor.shape),
        ],
        out_specs=once((1, rows, 128)),
        out_shape=jax.ShapeDtypeStruct((1, rows, 128), F32),
        scratch_shapes=[
            pltpu.VMEM((rows, 128), F32),
            pltpu.VMEM((angles, 3 * basis), BF16),
            pltpu.VMEM((basis, 3 * angles), BF16),
        ],
        compiler_params=pltpu.CompilerParams(vmem_limit_bytes=40 * MIB),
        cost_estimate=pl.CostEstimate(
            flops=8_000_000_000, bytes_accessed=16_000_000, transcendentals=0
        ),
        name="local_terms",
    )(sizes, centrifugal, x, previous, potential, legendre, stretch, inertia, factor)


def pair_product(matrix, pair):
    m = jnp.concatenate(pair, 1)
    high, low = halves(m)
    both = jnp.dot(matrix, jnp.concatenate([high, low], 0), preferred_element_type=F32)
    half = both.shape[0] // 2
    total = both[:half] + both[half:]
    return total[:, :128], total[:, 128:]


def radial_kernel(matrix_ref, x_ref, out_ref):
    peers, columns, rows, width = x_ref.shape
    for c in range(0, columns, 2):
        pair = [x_ref[:, c + k].reshape(peers * rows, width) for k in range(2)]
        for k, total in enumerate(pair_product(matrix_ref[...], pair)):
            out_ref[:, c + k] = total.reshape(peers, rows, width)


def radial_apply(matrix, received):
    peers, columns, rows, width = received.shape
    some = pl.BlockSpec((peers, 8, rows, width), lambda i: (0, i, 0, 0))
    return pl.pallas_call(
        radial_kernel,
        grid=(columns // 8,),
        in_specs=[pl.BlockSpec(matrix.shape, lambda i: (0, 0)), some],
        out_specs=some,
        out_shape=jax.ShapeDtypeStruct(received.shape, F32),
        cost_estimate=pl.CostEstimate(
            flops=columns * 20_000_000, bytes_accessed=2 * 4 * received.size, transcendentals=0
        ),
        name="radial_apply",
    )(matrix, received)


def radial_apart_kernel(where_ref, matrix_ref, *refs):
    *ours, theirs, out_theirs, turned = refs
    chips = len(ours) // 2
    ours, outs = ours[:chips], ours[chips:]
    columns, rows, width = theirs.shape[1:]

    @pl.when(pl.program_id(0) == 0)
    def _():
        size = matrix_ref.shape[0]
        i = lax.broadcasted_iota(jnp.int32, (size, size), 0)
        j = lax.broadcasted_iota(jnp.int32, (size, size), 1)
        moved = jnp.where(j == (i ^ (where_ref[0] * rows)), 1.0, 0.0).astype(BF16)
        half = jnp.dot(moved, matrix_ref[...], preferred_element_type=F32).astype(BF16)
        turned[...] = jnp.dot(half, moved, preferred_element_type=F32).astype(BF16)

    for c in range(0, columns, 2):
        pair = []
        for k in range(2):
            pieces = []
            for d in range(chips):
                pieces += [ours[d][0, c + k], theirs[d, c + k]]
            pair.append(jnp.concatenate(pieces, 0))
        for k, total in enumerate(pair_product(turned[...], pair)):
            for d in range(chips):
                at = 2 * d * rows
                outs[d][c + k] = total[at : at + rows]
                out_theirs[d, c + k] = total[at + rows : at + 2 * rows]


def radial_apart(where, matrix, ours, theirs):
    chips = len(ours)
    columns, rows, width = theirs.shape[1:]
    mine = pl.BlockSpec((1, 8, rows, width), lambda i, where: (where[1], i, 0, 0))
    made = pl.BlockSpec((8, rows, width), lambda i, where: (i, 0, 0))
    all_chips = pl.BlockSpec((chips, 8, rows, width), lambda i, where: (0, i, 0, 0))

    def kernel(where_ref, matrix_ref, *refs):
        ins, theirs_ref = refs[:chips], refs[chips]
        outs, out_theirs, turned = refs[chips + 1 : 2 * chips + 1], refs[-2], refs[-1]
        radial_apart_kernel(where_ref, matrix_ref, *ins, *outs, theirs_ref, out_theirs, turned)

    return pl.pallas_call(
        kernel,
        grid_spec=pltpu.PrefetchScalarGridSpec(
            num_scalar_prefetch=1,
            grid=(columns // 8,),
            in_specs=[pl.BlockSpec(matrix.shape, lambda i, where: (0, 0))]
            + [mine] * chips + [all_chips],
            out_specs=[made] * chips + [all_chips],
            scratch_shapes=[pltpu.VMEM(matrix.shape, BF16)],
        ),
        out_shape=[jax.ShapeDtypeStruct(theirs.shape[1:], F32)] * chips
        + [jax.ShapeDtypeStruct(theirs.shape, F32)],
        cost_estimate=pl.CostEstimate(
            flops=columns * 20_000_000, bytes_accessed=16 * theirs.size, transcendentals=0
        ),
        name="radial_apart",
    )(where, matrix, *ours, theirs)


def middle_kernel(
    sizes, coriolis, below_ref, above_ref, x_ref, lower_ref, upper_ref, inertia_ref, factor_ref, out_ref
):
    step = pl.program_id(0)
    radial = inertia_ref.shape[0]
    count = x_ref.shape[1] // radial
    both = 2.0 * factor_ref[...] * inertia_ref[...]
    below, above = sizes[0], sizes[1]

    @pl.loop(0, count // 4)
    def _(i):
        for k in range(4):
            local = i * 4 + k
            j = step * count + local
            at = pl.ds(pl.multiple_of(local * radial, radial), radial)
            here = jnp.where(j < below, x_ref[0, at, :], 0.0)
            there = jnp.where(j < above, x_ref[1, at, :], 0.0)
            low = coriolis[1, j] * there + coriolis[0, j] * lower_ref[at, :]
            high = coriolis[2, j] * upper_ref[at, :] + coriolis[1, j] * here
            out_ref[0, at, :] = below_ref[0, at, :] + jnp.where(j < below, both * low, 0.0)
            out_ref[1, at, :] = above_ref[0, at, :] + jnp.where(j < above, both * high, 0.0)


def middle_terms(sizes, coriolis, below, above, x, lower, upper, inertia, factor):
    blocks, rows, width = x.shape
    parts = 8
    smem = pl.BlockSpec(memory_space=pltpu.SMEM)
    pair = pl.BlockSpec((blocks, rows // parts, width), lambda i: (0, i, 0))
    single = pl.BlockSpec((1, rows // parts, width), lambda i: (0, i, 0))
    one = pl.BlockSpec((rows // parts, width), lambda i: (i, 0))
    small = pl.BlockSpec(inertia.shape, lambda i: (0, 0))
    return pl.pallas_call(
        middle_kernel,
        grid=(parts,),
        in_specs=[smem, smem, single, single, pair, one, one, small, small],
        out_specs=pair,
        out_shape=jax.ShapeDtypeStruct(x.shape, F32),
        compiler_params=pltpu.CompilerParams(vmem_limit_bytes=20 * MIB),
        cost_estimate=pl.CostEstimate(flops=30_000_000, bytes_accessed=25_000_000, transcendentals=0),
        name="middle_terms",
    )(sizes, coriolis, below, above, x, lower, upper, inertia, factor)


def add_rows(target, source, double, columns, begin, live):
    radial = double.shape[0]

    @pl.loop(0, columns // 8)
    def _(i):
        for k in range(8):
            j = i * 8 + k
            at = pl.ds(pl.multiple_of(j * radial, radial), radial)
            target(at, jnp.where(begin + j < live, double * source[at, :], 0.0))


def add_apart_kernel(basis, lead, where, sizes, out_in, factor_ref, *refs):
    backs, out_ref = refs[:-1], refs[-1]
    step = pl.program_id(0)
    part = out_in.shape[0] // 2
    columns = part // factor_ref.shape[0]
    begin = (lead + (where[0] // 2 ^ step)) * 2 * columns
    live = jnp.where(begin < basis, sizes[0], sizes[1] + basis)
    for d, back_ref in enumerate(backs):
        @pl.when(step == d)
        def _():
            for core in range(2):
                source = back_ref.at[pl.ds(pl.multiple_of((where[1] ^ core) * part, part), part), :]

                def target(at, more):
                    to = pl.ds(core * part + at.start, at.size)
                    out_ref[to, :] = out_in[to, :] + more

                add_rows(target, source, 2.0 * factor_ref[...], columns, begin + core * columns, live)


def add_apart(basis, lead, where, sizes, out, backs, factor):
    rows, width = backs[0].shape
    window = pl.BlockSpec((rows, width), lambda i, where, sizes: (lead + (where[0] // 2 ^ i), 0))
    full = lambda a: pl.BlockSpec(a.shape, lambda i, where, sizes: (0, 0))
    return pl.pallas_call(
        functools.partial(add_apart_kernel, basis, lead),
        grid_spec=pltpu.PrefetchScalarGridSpec(
            num_scalar_prefetch=2,
            grid=(len(backs),),
            in_specs=[window, full(factor)] + [full(b) for b in backs],
            out_specs=window,
        ),
        out_shape=jax.ShapeDtypeStruct(out.shape, F32),
        input_output_aliases={2: 0},
        compiler_params=pltpu.CompilerParams(vmem_limit_bytes=20 * MIB),
        cost_estimate=pl.CostEstimate(
            flops=1_000_000, bytes_accessed=12 * rows * width * len(backs), transcendentals=0
        ),
        name="add_apart",
    )(where, sizes, out, factor, *backs)


def add_joined_kernel(basis, sizes, out_in, back_ref, factor_ref, out_ref):
    columns = out_in.shape[0] // factor_ref.shape[0]
    begin = pl.program_id(0) * columns
    live = jnp.where(begin < basis, sizes[0], sizes[1] + basis)

    def target(at, more):
        out_ref[at, :] = out_in[at, :] + more

    add_rows(target, back_ref, 2.0 * factor_ref[...], columns, begin, live)


def add_joined(basis, sizes, out, back, factor):
    rows, width = back.shape
    part = 128 * factor.shape[0]
    some = pl.BlockSpec((part, width), lambda i: (i, 0))
    return pl.pallas_call(
        functools.partial(add_joined_kernel, basis),
        grid=(rows // part,),
        in_specs=[
            pl.BlockSpec(memory_space=pltpu.SMEM), some, some,
            pl.BlockSpec(factor.shape, lambda i: (0, 0)),
        ],
        out_specs=some,
        out_shape=jax.ShapeDtypeStruct(out.shape, F32),
        input_output_aliases={1: 0},
        compiler_params=pltpu.CompilerParams(vmem_limit_bytes=20 * MIB),
        cost_estimate=pl.CostEstimate(
            flops=1_000_000, bytes_accessed=12 * rows * width, transcendentals=0
        ),
        name="add_joined",
    )(sizes, out, back, factor)


def swap(x, by):
    peers = lax.axis_size("row")
    return lax.ppermute(x, "row", [(i, i ^ by) for i in range(peers)])


def after(x, *first):
    return lax.optimization_barrier((x, *first))[0]


def shards(
    packet, previous, basis_sizes, centrifugal, coriolis, inertia, damping,
    radial_kin, stretch_kin, legendre, potential,
):
    blocks, basis, radial, width = packet.shape
    peers = lax.axis_size("row")
    ka = lax.axis_index("ka")
    row = lax.axis_index("row")
    columns = blocks * basis
    rows = basis * radial
    joined = 2 * columns // 3
    piece = (columns - joined) // peers
    chips = peers // 2
    x_chip, core = row // 2, row % 2

    flat = packet.reshape(columns, radial, width)
    sent_a = flat[:joined]
    got_a = exchange(sent_a)
    source = after(flat, sent_a)
    sent = [
        lax.dynamic_slice_in_dim(source, joined + (x_chip ^ d) * 2 * piece, 2 * piece, 0)
        for d in range(chips)
    ]
    ours = [sent[0]] + [swap(sent[d], 2 * d) for d in range(1, chips)]
    live_mask = (lax.broadcasted_iota(jnp.int32, (blocks, basis), 1) < basis_sizes[:, None]).astype(F32)
    source = after(packet, *sent)
    upper = source[:1] * live_mask[:1, :, None, None]
    lower = source[1:] * live_mask[1:, :, None, None]
    from_ahead = from_behind(upper, "ka", -1)
    from_below = from_behind(lower, "ka", 1)

    inertia_local = lax.dynamic_slice_in_dim(inertia, row * radial, radial, 0)
    factor = jnp.broadcast_to(damping[:, None], (radial, width))
    t_high, t_low = halves_outside(radial_kin)
    t_high, t_low = [jnp.concatenate([t, t], 1) for t in (t_high, t_low)]
    matrix = jnp.concatenate([t_high, t_low], 0)
    s_high, s_low = halves_outside(stretch_kin.T)
    stretch = jnp.concatenate([jnp.concatenate([s_high, s_low], 1)] * 2, 0)
    start = jnp.maximum(ka * blocks - 1, 0)
    coupling = jnp.concatenate(
        [lax.dynamic_slice_in_dim(coriolis, start, 1, 0),
         lax.dynamic_slice_in_dim(coriolis, ka * blocks, blocks, 0)], 0
    )

    x = packet.reshape(blocks, rows, width)
    before = previous.reshape(blocks, rows, width)
    grid = potential.reshape(potential.shape[0] * radial, width)

    def local(block, x):
        return local_terms(
            block, basis_sizes, centrifugal, x, before, grid, legendre, stretch, inertia_local, factor
        )

    below = local(0, after(x, upper, lower))
    above = local(1, after(x, below))
    made_a = radial_apply(after(matrix, above), got_a.reshape(peers, joined // peers, radial, width))
    back_a = exchange(made_a.reshape(joined, radial, width))
    ours = lax.optimization_barrier((made_a, *ours))[1:]
    ours = [o.reshape(2, piece, radial, width) for o in ours]
    passed = [lax.dynamic_index_in_dim(o, 1 - core, 0) for o in ours]
    theirs = swap(jnp.concatenate(passed, 0), 1)
    where = jnp.stack([row, core]).astype(jnp.int32)
    *made_b, passed = radial_apart(where, after(matrix, made_a, from_ahead, from_below), ours, theirs)
    passed = swap(passed, 1)
    joint = [jnp.concatenate([made_b[d], passed[d]], 0) for d in range(chips)]
    back_b = [joint[0]] + [swap(joint[d], 2 * d) for d in range(1, chips)]

    upper = from_ahead.reshape(rows, width)
    lower = from_below.reshape(rows, width)
    out = middle_terms(
        basis_sizes, coupling, below, above, after(x, *joint), lower, upper, inertia_local, factor
    )
    out = out.reshape(columns * radial, width)
    out = add_joined(basis, basis_sizes, out, back_a.reshape(joined * radial, width), factor)
    out = add_apart(
        basis, joined // (2 * piece), where, basis_sizes, out,
        [b.reshape(2 * piece * radial, width) for b in back_b], factor,
    )
    return out.reshape(packet.shape)


def solution(mesh):
    in_specs = (
        P("ka", None, "row", None),
        P("ka", None, "row", None),
        P("ka"),
        P("ka", None),
        P(),
        P(),
        P("row"),
        P(),
        P(),
        P("ka", None, None),
        P(None, "row", None),
    )
    out_specs = P("ka", None, "row", None)
    return jax.shard_map(shards, mesh=mesh, in_specs=in_specs, out_specs=out_specs, check_vma=False)
```

```python
import functools

import jax
import jax.numpy as jnp
from jax import lax
from jax.experimental import pallas as pl
from jax.experimental.pallas import tpu as pltpu
from jax.sharding import PartitionSpec as P

F32 = jnp.float32
BF16 = jnp.bfloat16
MIB = 1 << 20
BRIEF = pl.CostEstimate(flops=1_000_000, bytes_accessed=100_000, transcendentals=0)


def from_behind(x, axis, by):
    peers = lax.axis_size(axis)
    pairs = [(i, i + by) for i in range(peers) if 0 <= i + by < peers]
    return lax.ppermute(x, axis, pairs)


def exchange(x):
    return lax.all_to_all(x, "row", split_axis=0, concat_axis=0, tiled=True)


def halves(x):
    high = x.astype(BF16)
    return high, (x - high.astype(F32)).astype(BF16)


def halves_outside(x):
    high = lax.reduce_precision(x, 8, 7)
    return high.astype(BF16), (x - high).astype(BF16)


def leading_kernel(x_ref, out_ref, held, come, go):
    parts, size = held.shape[:2]
    into = [
        pltpu.make_async_copy(x_ref.at[pl.ds(i * size, size)], held.at[i], come.at[i])
        for i in range(parts)
    ]
    onward = [
        pltpu.make_async_copy(held.at[i], out_ref.at[pl.ds(i * size, size)], go.at[i])
        for i in range(parts)
    ]
    for copy in into:
        copy.start()
    for i in range(parts):
        into[i].wait()
        onward[i].start()
    for copy in onward:
        copy.wait()


def leading(x, count):
    parts = 8
    return pl.pallas_call(
        leading_kernel,
        in_specs=[pl.BlockSpec(memory_space=pl.ANY)],
        out_specs=pl.BlockSpec(memory_space=pl.ANY),
        out_shape=jax.ShapeDtypeStruct((count, *x.shape[1:]), F32),
        scratch_shapes=[
            pltpu.VMEM((parts, count // parts, *x.shape[1:]), F32),
            pltpu.SemaphoreType.DMA((parts,)),
            pltpu.SemaphoreType.DMA((parts,)),
        ],
        cost_estimate=BRIEF,
        name="leading",
    )(x)


def local_kernel(
    block, sizes, centrifugal, x_ref, previous_ref, potential_ref, legendre_ref, stretch_ref,
    inertia_ref, factor_ref, out_ref, acc, ahead, back,
):
    live = sizes[block]
    angles, basis = legendre_ref.shape[1:]
    radial = inertia_ref.shape[0]
    rows = basis * radial
    high, low = halves(legendre_ref[0])
    ahead[:, :basis] = high
    ahead[:, basis : 2 * basis] = high
    ahead[:, 2 * basis :] = low
    high, low = halves(legendre_ref[0].T)
    back[:, :angles] = high
    back[:, angles : 2 * angles] = high
    back[:, 2 * angles :] = low

    piece = rows // 8

    @pl.loop(0, 8)
    def _(i):
        at = pl.ds(pl.multiple_of(i * piece, piece), piece)
        high, low = halves(x_ref[0, at, :])
        both = jnp.dot(
            jnp.concatenate([high, low], 1), stretch_ref[...], preferred_element_type=F32
        )
        acc[at, :] = both[:, :128] + both[:, 128:]

    mask = lax.broadcasted_iota(jnp.int32, (basis, 256), 0) < live

    @pl.loop(0, radial // 2)
    def _(i):
        r = 2 * i
        here = [pl.ds(r + k, basis, stride=radial) for k in range(2)]
        there = [pl.ds(r + k, angles, stride=radial) for k in range(2)]
        m = jnp.concatenate([x_ref[0, at, :] for at in here], 1)
        m = jnp.where(mask, m, 0.0)
        high, low = halves(m)
        grid = jnp.dot(
            ahead[...], jnp.concatenate([high, low, high], 0), preferred_element_type=F32
        )
        grid = grid * jnp.concatenate([potential_ref[at, :] for at in there], 1)
        high, low = halves(grid)
        term = jnp.dot(
            back[...], jnp.concatenate([high, low, high], 0), preferred_element_type=F32
        )
        for k in range(2):
            acc[here[k], :] += term[:, 128 * k : 128 * (k + 1)]

    inertia = inertia_ref[...]
    factor = factor_ref[...]

    @pl.loop(0, basis // 8)
    def _(i):
        for k in range(8):
            j = i * 8 + k
            at = pl.ds(pl.multiple_of(j * radial, radial), radial)
            value = acc[at, :] + (centrifugal[block, j] * inertia) * x_ref[0, at, :]
            value = factor * (2.0 * value - factor * previous_ref[0, at, :])
            out_ref[0, at, :] = jnp.where(j < live, value, 0.0)


def local_terms(block, sizes, centrifugal, x, previous, potential, legendre, stretch, inertia, factor):
    angles, basis = legendre.shape[1:]
    rows = x.shape[1]
    whole = pl.BlockSpec((1, rows, 128), lambda k: (block, 0, 0))
    smem = pl.BlockSpec(memory_space=pltpu.SMEM)
    once = lambda shape: pl.BlockSpec(shape, lambda k: (0,) * len(shape))
    return pl.pallas_call(
        functools.partial(local_kernel, block),
        grid=(1,),
        in_specs=[
            smem, smem, whole, whole, once(potential.shape),
            pl.BlockSpec((1, angles, basis), lambda k: (block, 0, 0)),
            once(stretch.shape), once(inertia.shape), once(factor.shape),
        ],
        out_specs=once((1, rows, 128)),
        out_shape=jax.ShapeDtypeStruct((1, rows, 128), F32),
        scratch_shapes=[
            pltpu.VMEM((rows, 128), F32),
            pltpu.VMEM((angles, 3 * basis), BF16),
            pltpu.VMEM((basis, 3 * angles), BF16),
        ],
        compiler_params=pltpu.CompilerParams(vmem_limit_bytes=40 * MIB),
        cost_estimate=BRIEF,
        name="local_terms",
    )(sizes, centrifugal, x, previous, potential, legendre, stretch, inertia, factor)


def pair_product(matrix, pair):
    m = jnp.concatenate(pair, 1)
    high, low = halves(m)
    both = jnp.dot(matrix, jnp.concatenate([high, low], 0), preferred_element_type=F32)
    half = both.shape[0] // 2
    total = both[:half] + both[half:]
    return total[:, :128], total[:, 128:]


def radial_kernel(matrix_ref, x_ref, out_ref):
    peers, columns, rows, width = x_ref.shape
    for c in range(0, columns, 2):
        pair = [x_ref[:, c + k].reshape(peers * rows, width) for k in range(2)]
        for k, total in enumerate(pair_product(matrix_ref[...], pair)):
            out_ref[:, c + k] = total.reshape(peers, rows, width)


def radial_apply(matrix, received):
    peers, columns, rows, width = received.shape
    some = pl.BlockSpec((peers, 8, rows, width), lambda i: (0, i, 0, 0))
    return pl.pallas_call(
        radial_kernel,
        grid=(columns // 8,),
        in_specs=[pl.BlockSpec(matrix.shape, lambda i: (0, 0)), some],
        out_specs=some,
        out_shape=jax.ShapeDtypeStruct(received.shape, F32),
        cost_estimate=BRIEF,
        name="radial_apply",
    )(matrix, received)


def radial_apart_kernel(where_ref, matrix_ref, *refs):
    *ours, theirs, out_theirs, turned = refs
    chips = len(ours) // 2
    ours, outs = ours[:chips], ours[chips:]
    columns, rows, width = theirs.shape[1:]

    @pl.when(pl.program_id(0) == 0)
    def _():
        size = matrix_ref.shape[0]
        i = lax.broadcasted_iota(jnp.int32, (size, size), 0)
        j = lax.broadcasted_iota(jnp.int32, (size, size), 1)
        moved = jnp.where(j == (i ^ (where_ref[0] * rows)), 1.0, 0.0).astype(BF16)
        half = jnp.dot(moved, matrix_ref[...], preferred_element_type=F32).astype(BF16)
        turned[...] = jnp.dot(half, moved, preferred_element_type=F32).astype(BF16)

    for c in range(0, columns, 2):
        pair = []
        for k in range(2):
            pieces = []
            for d in range(chips):
                pieces += [ours[d][0, c + k], theirs[d, c + k]]
            pair.append(jnp.concatenate(pieces, 0))
        for k, total in enumerate(pair_product(turned[...], pair)):
            for d in range(chips):
                at = 2 * d * rows
                outs[d][c + k] = total[at : at + rows]
                out_theirs[d, c + k] = total[at + rows : at + 2 * rows]


def radial_apart(where, matrix, ours, theirs):
    chips = len(ours)
    columns, rows, width = theirs.shape[1:]
    mine = pl.BlockSpec((1, 8, rows, width), lambda i, where: (where[1], i, 0, 0))
    made = pl.BlockSpec((8, rows, width), lambda i, where: (i, 0, 0))
    all_chips = pl.BlockSpec((chips, 8, rows, width), lambda i, where: (0, i, 0, 0))

    def kernel(where_ref, matrix_ref, *refs):
        ins, theirs_ref = refs[:chips], refs[chips]
        outs, out_theirs, turned = refs[chips + 1 : 2 * chips + 1], refs[-2], refs[-1]
        radial_apart_kernel(where_ref, matrix_ref, *ins, *outs, theirs_ref, out_theirs, turned)

    return pl.pallas_call(
        kernel,
        grid_spec=pltpu.PrefetchScalarGridSpec(
            num_scalar_prefetch=1,
            grid=(columns // 8,),
            in_specs=[pl.BlockSpec(matrix.shape, lambda i, where: (0, 0))]
            + [mine] * chips + [all_chips],
            out_specs=[made] * chips + [all_chips],
            scratch_shapes=[pltpu.VMEM(matrix.shape, BF16)],
        ),
        out_shape=[jax.ShapeDtypeStruct(theirs.shape[1:], F32)] * chips
        + [jax.ShapeDtypeStruct(theirs.shape, F32)],
        cost_estimate=BRIEF,
        name="radial_apart",
    )(where, matrix, *ours, theirs)


def middle_kernel(
    sizes, coriolis, below_ref, above_ref, x_ref, lower_ref, upper_ref, first_ref, second_ref,
    inertia_ref, factor_ref, out_ref
):
    step = pl.program_id(0)
    radial = inertia_ref.shape[0]
    count = x_ref.shape[1] // radial
    double = 2.0 * factor_ref[...]
    inertia = inertia_ref[...]
    below, above = sizes[0], sizes[1]

    def part(more):
        @pl.loop(0, count // 4)
        def _(i):
            for k in range(4):
                local = i * 4 + k
                j = step * count + local
                at = pl.ds(pl.multiple_of(local * radial, radial), radial)
                here = jnp.where(j < below, x_ref[0, at, :], 0.0)
                there = jnp.where(j < above, x_ref[1, at, :], 0.0)
                low = coriolis[1, j] * there + coriolis[0, j] * lower_ref[at, :]
                high = coriolis[2, j] * upper_ref[at, :] + coriolis[1, j] * here
                low = double * (inertia * low + first_ref[at, :])
                high = inertia * high
                if more:
                    high = high + second_ref[at, :]
                high = double * high
                out_ref[0, at, :] = below_ref[0, at, :] + jnp.where(j < below, low, 0.0)
                out_ref[1, at, :] = above_ref[0, at, :] + jnp.where(j < above, high, 0.0)

    pl.when(step < SECOND_PARTS)(lambda: part(True))
    pl.when(step >= SECOND_PARTS)(lambda: part(False))


MIDDLE_PARTS = 12
SECOND_PARTS = 4


def middle_terms(sizes, coriolis, below, above, x, lower, upper, back, inertia, factor):
    blocks, rows, width = x.shape
    size = rows // MIDDLE_PARTS
    assert back.shape[0] == rows + size * SECOND_PARTS
    smem = pl.BlockSpec(memory_space=pltpu.SMEM)
    pair = pl.BlockSpec((blocks, size, width), lambda i: (0, i, 0))
    single = pl.BlockSpec((1, size, width), lambda i: (0, i, 0))
    one = pl.BlockSpec((size, width), lambda i: (i, 0))
    second = pl.BlockSpec((size, width), lambda i: (MIDDLE_PARTS + jnp.minimum(i, SECOND_PARTS - 1), 0))
    small = pl.BlockSpec(inertia.shape, lambda i: (0, 0))
    return pl.pallas_call(
        middle_kernel,
        grid=(MIDDLE_PARTS,),
        in_specs=[smem, smem, single, single, pair, one, one, one, second, small, small],
        out_specs=pair,
        out_shape=jax.ShapeDtypeStruct(x.shape, F32),
        compiler_params=pltpu.CompilerParams(vmem_limit_bytes=20 * MIB),
        cost_estimate=BRIEF,
        name="middle_terms",
    )(sizes, coriolis, below, above, x, lower, upper, back, back, inertia, factor)


def add_rows(target, source, double, columns, begin, live):
    radial = double.shape[0]

    @pl.loop(0, columns // 8)
    def _(i):
        for k in range(8):
            j = i * 8 + k
            at = pl.ds(pl.multiple_of(j * radial, radial), radial)
            target(at, jnp.where(begin + j < live, double * source[at, :], 0.0))


def add_apart_kernel(basis, lead, where, sizes, out_in, factor_ref, *refs):
    backs, out_ref = refs[:-1], refs[-1]
    step = pl.program_id(0)
    part = out_in.shape[0] // 2
    columns = part // factor_ref.shape[0]
    begin = (lead + (where[0] // 2 ^ step)) * 2 * columns
    live = jnp.where(begin < basis, sizes[0], sizes[1] + basis)
    for d, back_ref in enumerate(backs):
        @pl.when(step == d)
        def _():
            for core in range(2):
                source = back_ref.at[pl.ds(pl.multiple_of((where[1] ^ core) * part, part), part), :]

                def target(at, more):
                    to = pl.ds(core * part + at.start, at.size)
                    out_ref[to, :] = out_in[to, :] + more

                add_rows(target, source, 2.0 * factor_ref[...], columns, begin + core * columns, live)


def add_apart(basis, lead, where, sizes, out, backs, factor):
    rows, width = backs[0].shape
    window = pl.BlockSpec((rows, width), lambda i, where, sizes: (lead + (where[0] // 2 ^ i), 0))
    full = lambda a: pl.BlockSpec(a.shape, lambda i, where, sizes: (0, 0))
    return pl.pallas_call(
        functools.partial(add_apart_kernel, basis, lead),
        grid_spec=pltpu.PrefetchScalarGridSpec(
            num_scalar_prefetch=2,
            grid=(len(backs),),
            in_specs=[window, full(factor)] + [full(b) for b in backs],
            out_specs=window,
        ),
        out_shape=jax.ShapeDtypeStruct(out.shape, F32),
        input_output_aliases={2: 0},
        compiler_params=pltpu.CompilerParams(vmem_limit_bytes=20 * MIB),
        cost_estimate=BRIEF,
        name="add_apart",
    )(where, sizes, out, factor, *backs)


def swap(x, by):
    peers = lax.axis_size("row")
    return lax.ppermute(x, "row", [(i, i ^ by) for i in range(peers)])


def after(x, *first):
    return lax.optimization_barrier((x, *first))[0]


def shards(
    packet, previous, basis_sizes, centrifugal, coriolis, inertia, damping,
    radial_kin, stretch_kin, legendre, potential,
):
    blocks, basis, radial, width = packet.shape
    peers = lax.axis_size("row")
    ka = lax.axis_index("ka")
    row = lax.axis_index("row")
    columns = blocks * basis
    rows = basis * radial
    joined = 2 * columns // 3
    piece = (columns - joined) // peers
    chips = peers // 2
    x_chip, core = row // 2, row % 2

    flat = packet.reshape(columns, radial, width)
    sent_a = leading(flat, joined)
    got_a = exchange(sent_a)
    source = after(flat, sent_a)
    sent = [
        lax.dynamic_slice_in_dim(source, joined + (x_chip ^ d) * 2 * piece, 2 * piece, 0)
        for d in range(chips)
    ]
    ours = [sent[0]] + [swap(sent[d], 2 * d) for d in range(1, chips)]
    live_mask = (lax.broadcasted_iota(jnp.int32, (blocks, basis), 1) < basis_sizes[:, None]).astype(F32)
    source = after(packet, *sent)
    upper = source[:1] * live_mask[:1, :, None, None]
    lower = source[1:] * live_mask[1:, :, None, None]
    from_ahead = from_behind(upper, "ka", -1)
    from_below = from_behind(lower, "ka", 1)

    inertia_local = lax.dynamic_slice_in_dim(inertia, row * radial, radial, 0)
    factor = jnp.broadcast_to(damping[:, None], (radial, width))
    t_high, t_low = halves_outside(radial_kin)
    t_high, t_low = [jnp.concatenate([t, t], 1) for t in (t_high, t_low)]
    matrix = jnp.concatenate([t_high, t_low], 0)
    s_high, s_low = halves_outside(stretch_kin.T)
    stretch = jnp.concatenate([jnp.concatenate([s_high, s_low], 1)] * 2, 0)
    start = jnp.maximum(ka * blocks - 1, 0)
    coupling = jnp.concatenate(
        [lax.dynamic_slice_in_dim(coriolis, start, 1, 0),
         lax.dynamic_slice_in_dim(coriolis, ka * blocks, blocks, 0)], 0
    )

    x = packet.reshape(blocks, rows, width)
    before = previous.reshape(blocks, rows, width)
    grid = potential.reshape(potential.shape[0] * radial, width)

    def local(block, x):
        return local_terms(
            block, basis_sizes, centrifugal, x, before, grid, legendre, stretch, inertia_local, factor
        )

    below = local(0, after(x, upper, lower))
    made_a = radial_apply(after(matrix, below), got_a.reshape(peers, joined // peers, radial, width))
    back_a = exchange(made_a.reshape(joined, radial, width))
    ours = lax.optimization_barrier((made_a, *ours))[1:]
    above = local(1, after(x, *ours))
    ours = [o.reshape(2, piece, radial, width) for o in ours]
    passed = [lax.dynamic_index_in_dim(o, 1 - core, 0) for o in ours]
    theirs = swap(jnp.concatenate(passed, 0), 1)
    where = jnp.stack([row, core]).astype(jnp.int32)
    *made_b, passed = radial_apart(where, after(matrix, above, from_ahead, from_below), ours, theirs)
    passed = swap(passed, 1)
    joint = [jnp.concatenate([made_b[d], passed[d]], 0) for d in range(chips)]
    back_b = [joint[0]] + [swap(joint[d], 2 * d) for d in range(1, chips)]

    upper = from_ahead.reshape(rows, width)
    lower = from_below.reshape(rows, width)
    out = middle_terms(
        basis_sizes, coupling, below, above, x, lower, upper,
        back_a.reshape(joined * radial, width), inertia_local, factor,
    )
    out = out.reshape(columns * radial, width)
    out = add_apart(
        basis, joined // (2 * piece), where, basis_sizes, out,
        [b.reshape(2 * piece * radial, width) for b in back_b], factor,
    )
    return out.reshape(packet.shape)


def solution(mesh):
    in_specs = (
        P("ka", None, "row", None),
        P("ka", None, "row", None),
        P("ka"),
        P("ka", None),
        P(),
        P(),
        P("row"),
        P(),
        P(),
        P("ka", None, None),
        P(None, "row", None),
    )
    out_specs = P("ka", None, "row", None)
    return jax.shard_map(shards, mesh=mesh, in_specs=in_specs, out_specs=out_specs, check_vma=False)
```

```python
import functools

import jax
import jax.numpy as jnp
from jax import lax
from jax.experimental import pallas as pl
from jax.experimental.pallas import tpu as pltpu
from jax.sharding import PartitionSpec as P

F32 = jnp.float32
BF16 = jnp.bfloat16
MIB = 1 << 20
BRIEF = pl.CostEstimate(flops=1, bytes_accessed=1, transcendentals=0)


def from_behind(x, axis, by):
    peers = lax.axis_size(axis)
    pairs = [(i, i + by) for i in range(peers) if 0 <= i + by < peers]
    return lax.ppermute(x, axis, pairs)


def exchange(x):
    return lax.all_to_all(x, "row", split_axis=0, concat_axis=0, tiled=True)


def halves(x):
    high = x.astype(BF16)
    return high, (x - high.astype(F32)).astype(BF16)


def halves_outside(x):
    high = lax.reduce_precision(x, 8, 7)
    return high.astype(BF16), (x - high).astype(BF16)


def leading_kernel(x_ref, out_ref, held, come, go):
    parts, size = held.shape[:2]
    into = [
        pltpu.make_async_copy(x_ref.at[pl.ds(i * size, size)], held.at[i], come.at[i])
        for i in range(parts)
    ]
    onward = [
        pltpu.make_async_copy(held.at[i], out_ref.at[pl.ds(i * size, size)], go.at[i])
        for i in range(parts)
    ]
    for copy in into:
        copy.start()
    for i in range(parts):
        into[i].wait()
        onward[i].start()
    for copy in onward:
        copy.wait()


def leading(x, count):
    parts = 4
    return pl.pallas_call(
        leading_kernel,
        in_specs=[pl.BlockSpec(memory_space=pl.ANY)],
        out_specs=pl.BlockSpec(memory_space=pl.ANY),
        out_shape=jax.ShapeDtypeStruct((count, *x.shape[1:]), F32),
        scratch_shapes=[
            pltpu.VMEM((parts, count // parts, *x.shape[1:]), F32),
            pltpu.SemaphoreType.DMA((parts,)),
            pltpu.SemaphoreType.DMA((parts,)),
        ],
        cost_estimate=BRIEF,
        name="leading",
    )(x)


def local_kernel(
    block, sizes, centrifugal, x_ref, previous_ref, potential_ref, legendre_ref, stretch_ref,
    inertia_ref, factor_ref, out_ref, acc, ahead, back,
):
    live = sizes[block]
    angles, basis = legendre_ref.shape[1:]
    radial = inertia_ref.shape[0]
    rows = basis * radial
    high, low = halves(legendre_ref[0])
    ahead[:, :basis] = high
    ahead[:, basis : 2 * basis] = high
    ahead[:, 2 * basis :] = low
    high, low = halves(legendre_ref[0].T)
    back[:, :angles] = high
    back[:, angles : 2 * angles] = high
    back[:, 2 * angles :] = low

    piece = rows // 8

    @pl.loop(0, 8)
    def _(i):
        at = pl.ds(pl.multiple_of(i * piece, piece), piece)
        high, low = halves(x_ref[0, at, :])
        both = jnp.dot(
            jnp.concatenate([high, low], 1), stretch_ref[...], preferred_element_type=F32
        )
        acc[at, :] = both[:, :128] + both[:, 128:]

    mask = lax.broadcasted_iota(jnp.int32, (basis, 256), 0) < live

    @pl.loop(0, radial // 2)
    def _(i):
        r = 2 * i
        here = [pl.ds(r + k, basis, stride=radial) for k in range(2)]
        there = [pl.ds(r + k, angles, stride=radial) for k in range(2)]
        m = jnp.concatenate([x_ref[0, at, :] for at in here], 1)
        m = jnp.where(mask, m, 0.0)
        high, low = halves(m)
        grid = jnp.dot(
            ahead[...], jnp.concatenate([high, low, high], 0), preferred_element_type=F32
        )
        grid = grid * jnp.concatenate([potential_ref[at, :] for at in there], 1)
        high, low = halves(grid)
        term = jnp.dot(
            back[...], jnp.concatenate([high, low, high], 0), preferred_element_type=F32
        )
        for k in range(2):
            acc[here[k], :] += term[:, 128 * k : 128 * (k + 1)]

    inertia = inertia_ref[...]
    factor = factor_ref[...]

    @pl.loop(0, basis // 8)
    def _(i):
        for k in range(8):
            j = i * 8 + k
            at = pl.ds(pl.multiple_of(j * radial, radial), radial)
            value = acc[at, :] + (centrifugal[block, j] * inertia) * x_ref[0, at, :]
            value = factor * (2.0 * value - factor * previous_ref[0, at, :])
            out_ref[0, at, :] = jnp.where(j < live, value, 0.0)


def local_terms(block, sizes, centrifugal, x, previous, potential, legendre, stretch, inertia, factor):
    angles, basis = legendre.shape[1:]
    rows = x.shape[1]
    whole = pl.BlockSpec((1, rows, 128), lambda k: (block, 0, 0))
    smem = pl.BlockSpec(memory_space=pltpu.SMEM)
    once = lambda shape: pl.BlockSpec(shape, lambda k: (0,) * len(shape))
    return pl.pallas_call(
        functools.partial(local_kernel, block),
        grid=(1,),
        in_specs=[
            smem, smem, whole, whole, once(potential.shape),
            pl.BlockSpec((1, angles, basis), lambda k: (block, 0, 0)),
            once(stretch.shape), once(inertia.shape), once(factor.shape),
        ],
        out_specs=once((1, rows, 128)),
        out_shape=jax.ShapeDtypeStruct((1, rows, 128), F32),
        scratch_shapes=[
            pltpu.VMEM((rows, 128), F32),
            pltpu.VMEM((angles, 3 * basis), BF16),
            pltpu.VMEM((basis, 3 * angles), BF16),
        ],
        compiler_params=pltpu.CompilerParams(vmem_limit_bytes=60 * MIB),
        cost_estimate=BRIEF,
        name="local_terms",
    )(sizes, centrifugal, x, previous, potential, legendre, stretch, inertia, factor)


def pair_product(matrix, pair):
    m = jnp.concatenate(pair, 1)
    high, low = halves(m)
    both = jnp.dot(matrix, jnp.concatenate([high, low], 0), preferred_element_type=F32)
    half = both.shape[0] // 2
    total = both[:half] + both[half:]
    return total[:, :128], total[:, 128:]


def radial_kernel(matrix_ref, x_ref, out_ref):
    peers, columns, rows, width = x_ref.shape
    for c in range(0, columns, 2):
        pair = [x_ref[:, c + k].reshape(peers * rows, width) for k in range(2)]
        for k, total in enumerate(pair_product(matrix_ref[...], pair)):
            out_ref[:, c + k] = total.reshape(peers, rows, width)


def radial_apply(matrix, received):
    peers, columns, rows, width = received.shape
    some = pl.BlockSpec((peers, 16, rows, width), lambda i: (0, i, 0, 0))
    return pl.pallas_call(
        radial_kernel,
        grid=(columns // 16,),
        in_specs=[pl.BlockSpec(matrix.shape, lambda i: (0, 0)), some],
        out_specs=some,
        out_shape=jax.ShapeDtypeStruct(received.shape, F32),
        compiler_params=pltpu.CompilerParams(vmem_limit_bytes=60 * MIB),
        cost_estimate=BRIEF,
        name="radial_apply",
    )(matrix, received)


def radial_apart_kernel(where_ref, matrix_ref, *refs):
    *ours, theirs, out_theirs, turned = refs
    chips = len(ours) // 2
    ours, outs = ours[:chips], ours[chips:]
    columns, rows, width = theirs.shape[1:]

    @pl.when(pl.program_id(0) == 0)
    def _():
        size = matrix_ref.shape[0]
        i = lax.broadcasted_iota(jnp.int32, (size, size), 0)
        j = lax.broadcasted_iota(jnp.int32, (size, size), 1)
        moved = jnp.where(j == (i ^ (where_ref[0] * rows)), 1.0, 0.0).astype(BF16)
        half = jnp.dot(moved, matrix_ref[...], preferred_element_type=F32).astype(BF16)
        turned[...] = jnp.dot(half, moved, preferred_element_type=F32).astype(BF16)

    for c in range(0, columns, 2):
        pair = []
        for k in range(2):
            pieces = []
            for d in range(chips):
                pieces += [ours[d][0, c + k], theirs[d, c + k]]
            pair.append(jnp.concatenate(pieces, 0))
        for k, total in enumerate(pair_product(turned[...], pair)):
            for d in range(chips):
                at = 2 * d * rows
                outs[d][c + k] = total[at : at + rows]
                out_theirs[d, c + k] = total[at + rows : at + 2 * rows]


def radial_apart(where, matrix, ours, theirs):
    chips = len(ours)
    columns, rows, width = theirs.shape[1:]
    mine = pl.BlockSpec((1, 8, rows, width), lambda i, where: (where[1], i, 0, 0))
    made = pl.BlockSpec((8, rows, width), lambda i, where: (i, 0, 0))
    all_chips = pl.BlockSpec((chips, 8, rows, width), lambda i, where: (0, i, 0, 0))

    def kernel(where_ref, matrix_ref, *refs):
        ins, theirs_ref = refs[:chips], refs[chips]
        outs, out_theirs, turned = refs[chips + 1 : 2 * chips + 1], refs[-2], refs[-1]
        radial_apart_kernel(where_ref, matrix_ref, *ins, *outs, theirs_ref, out_theirs, turned)

    return pl.pallas_call(
        kernel,
        grid_spec=pltpu.PrefetchScalarGridSpec(
            num_scalar_prefetch=1,
            grid=(columns // 8,),
            in_specs=[pl.BlockSpec(matrix.shape, lambda i, where: (0, 0))]
            + [mine] * chips + [all_chips],
            out_specs=[made] * chips + [all_chips],
            scratch_shapes=[pltpu.VMEM(matrix.shape, BF16)],
        ),
        out_shape=[jax.ShapeDtypeStruct(theirs.shape[1:], F32)] * chips
        + [jax.ShapeDtypeStruct(theirs.shape, F32)],
        cost_estimate=BRIEF,
        name="radial_apart",
    )(where, matrix, *ours, theirs)


def middle_kernel(
    sizes, coriolis, where, below_ref, above_ref, x_ref, lower_ref, upper_ref, first_ref, second_ref,
    own_ref, inertia_ref, factor_ref, out_ref
):
    step = pl.program_id(0)
    radial = inertia_ref.shape[0]
    count = x_ref.shape[1] // radial
    double = 2.0 * factor_ref[...]
    inertia = inertia_ref[...]
    below, above = sizes[0], sizes[1]

    def part(more):
        @pl.loop(0, count // 4)
        def _(i):
            for k in range(4):
                local = i * 4 + k
                j = step * count + local
                at = pl.ds(pl.multiple_of(local * radial, radial), radial)
                here = jnp.where(j < below, x_ref[0, at, :], 0.0)
                there = jnp.where(j < above, x_ref[1, at, :], 0.0)
                low = coriolis[1, j] * there + coriolis[0, j] * lower_ref[at, :]
                high = coriolis[2, j] * upper_ref[at, :] + coriolis[1, j] * here
                low = double * (inertia * low + first_ref[at, :])
                high = inertia * high
                if more:
                    high = high + second_ref[at, :]
                high = double * high
                out_ref[0, at, :] = below_ref[0, at, :] + jnp.where(j < below, low, 0.0)
                out_ref[1, at, :] = above_ref[0, at, :] + jnp.where(j < above, high, 0.0)

    pl.when(step < SECOND_PARTS)(lambda: part(True))
    pl.when(step >= SECOND_PARTS)(lambda: part(False))
    own = SECOND_PARTS + where[0] // 2 * 2

    @pl.when((step == own) | (step == own + 1))
    def _():
        start = ((step - own) ^ where[1]) * count

        @pl.loop(0, count // 4)
        def _(i):
            for k in range(4):
                local = i * 4 + k
                at = pl.ds(pl.multiple_of(local * radial, radial), radial)
                of = pl.ds(pl.multiple_of((start + local) * radial, radial), radial)
                more = jnp.where(step * count + local < above, double * own_ref[of, :], 0.0)
                out_ref[1, at, :] += more


MIDDLE_PARTS = 12
SECOND_PARTS = 4


def middle_terms(
    sizes, coriolis, where, below, above, x, lower, upper, back, own, inertia, factor
):
    blocks, rows, width = x.shape
    size = rows // MIDDLE_PARTS
    assert back.shape[0] == rows + size * SECOND_PARTS and own.shape[0] == 2 * size
    smem = pl.BlockSpec(memory_space=pltpu.SMEM)
    pair = pl.BlockSpec((blocks, size, width), lambda i: (0, i, 0))
    single = pl.BlockSpec((1, size, width), lambda i: (0, i, 0))
    one = pl.BlockSpec((size, width), lambda i: (i, 0))
    second = pl.BlockSpec((size, width), lambda i: (MIDDLE_PARTS + jnp.minimum(i, SECOND_PARTS - 1), 0))
    small = pl.BlockSpec(inertia.shape, lambda i: (0, 0))
    return pl.pallas_call(
        middle_kernel,
        grid=(MIDDLE_PARTS,),
        in_specs=[
            smem, smem, smem, single, single, pair, one, one, one, second,
            pl.BlockSpec(own.shape, lambda i: (0, 0)), small, small,
        ],
        out_specs=pair,
        out_shape=jax.ShapeDtypeStruct(x.shape, F32),
        compiler_params=pltpu.CompilerParams(vmem_limit_bytes=60 * MIB),
        cost_estimate=BRIEF,
        name="middle_terms",
    )(sizes, coriolis, where, below, above, x, lower, upper, back, back, own, inertia, factor)


def add_apart_kernel(basis, lead, where, sizes, out_in, factor_ref, *refs):
    backs, (out_ref, held, sems, end_sems) = refs[:-4], refs[-4:]
    radial = factor_ref.shape[0]
    rows = held.shape[1]
    columns = rows // radial
    half = columns // 2
    double = 2.0 * factor_ref[...]
    places = [lead + (where[0] // 2 ^ (i + 1)) for i in range(len(backs))]
    windows = [out_ref.at[pl.ds(pl.multiple_of(p * rows, rows), rows), :] for p in places]
    reads = [
        pltpu.make_async_copy(w, held.at[i], sems.at[i]) for i, w in enumerate(windows)
    ]
    writes = [
        pltpu.make_async_copy(held.at[i], w, end_sems.at[i]) for i, w in enumerate(windows)
    ]
    for read in reads:
        read.start()
    for i in range(len(backs)):
        reads[i].wait()
        begin = places[i] * columns
        live = jnp.where(begin < basis, sizes[0], sizes[1] + basis) - begin
        for core in range(2):
            shift = (where[1] ^ core) - core

            @pl.loop(0, half // 8)
            def _(c):
                for k in range(8):
                    j = core * half + c * 8 + k
                    at = pl.ds(pl.multiple_of(j * radial, radial), radial)
                    of = pl.ds(pl.multiple_of((j + shift * half) * radial, radial), radial)
                    held[i, at, :] += jnp.where(j < live, double * backs[i][of, :], 0.0)
        writes[i].start()
    for write in writes:
        write.wait()


def add_apart(basis, lead, where, sizes, out, backs, factor):
    rows, width = backs[0].shape
    count = len(backs)
    smem = pl.BlockSpec(memory_space=pltpu.SMEM)
    whole = pl.BlockSpec(memory_space=pl.ANY)
    return pl.pallas_call(
        functools.partial(add_apart_kernel, basis, lead),
        in_specs=[smem, smem, whole] + [pl.BlockSpec(memory_space=pltpu.VMEM)] * (1 + count),
        out_specs=whole,
        out_shape=jax.ShapeDtypeStruct(out.shape, F32),
        input_output_aliases={2: 0},
        scratch_shapes=[
            pltpu.VMEM((count, rows, width), F32),
            pltpu.SemaphoreType.DMA((count,)),
            pltpu.SemaphoreType.DMA((count,)),
        ],
        compiler_params=pltpu.CompilerParams(vmem_limit_bytes=16 * MIB),
        cost_estimate=BRIEF,
        name="add_apart",
    )(where, sizes, out, factor, *backs)


def swap(x, by):
    peers = lax.axis_size("row")
    return lax.ppermute(x, "row", [(i, i ^ by) for i in range(peers)])


def after(x, *first):
    return lax.optimization_barrier((x, *first))[0]


def shards(
    packet, previous, basis_sizes, centrifugal, coriolis, inertia, damping,
    radial_kin, stretch_kin, legendre, potential,
):
    blocks, basis, radial, width = packet.shape
    peers = lax.axis_size("row")
    ka = lax.axis_index("ka")
    row = lax.axis_index("row")
    columns = blocks * basis
    rows = basis * radial
    joined = 2 * columns // 3
    piece = (columns - joined) // peers
    chips = peers // 2
    x_chip, core = row // 2, row % 2

    flat = packet.reshape(columns, radial, width)
    def part(x, d):
        return lax.dynamic_slice_in_dim(x, joined + (x_chip ^ d) * 2 * piece, 2 * piece, 0)

    sent_a = leading(flat, joined)
    got_a = exchange(sent_a)
    source = after(flat, sent_a)
    sent = [part(source, d) for d in range(chips)]
    ours = [sent[0]] + [swap(sent[d], 2 * d) for d in range(1, chips)]
    live_mask = (lax.broadcasted_iota(jnp.int32, (blocks, basis), 1) < basis_sizes[:, None]).astype(F32)
    source = after(packet, *sent)
    upper = source[:1] * live_mask[:1, :, None, None]
    lower = source[1:] * live_mask[1:, :, None, None]
    from_ahead = from_behind(upper, "ka", -1)
    from_below = from_behind(lower, "ka", 1)

    inertia_local = lax.dynamic_slice_in_dim(inertia, row * radial, radial, 0)
    factor = jnp.broadcast_to(damping[:, None], (radial, width))
    t_high, t_low = halves_outside(radial_kin)
    t_high, t_low = [jnp.concatenate([t, t], 1) for t in (t_high, t_low)]
    matrix = jnp.concatenate([t_high, t_low], 0)
    s_high, s_low = halves_outside(stretch_kin.T)
    stretch = jnp.concatenate([jnp.concatenate([s_high, s_low], 1)] * 2, 0)
    start = jnp.maximum(ka * blocks - 1, 0)
    coupling = jnp.concatenate(
        [lax.dynamic_slice_in_dim(coriolis, start, 1, 0),
         lax.dynamic_slice_in_dim(coriolis, ka * blocks, blocks, 0)], 0
    )

    x = packet.reshape(blocks, rows, width)
    before = previous.reshape(blocks, rows, width)
    grid = potential.reshape(potential.shape[0] * radial, width)

    def local(block, x):
        return local_terms(
            block, basis_sizes, centrifugal, x, before, grid, legendre, stretch, inertia_local, factor
        )

    below = local(0, after(x, upper, lower))
    made_a = radial_apply(after(matrix, below), got_a.reshape(peers, joined // peers, radial, width))
    back_a = exchange(made_a.reshape(joined, radial, width))
    above = local(1, after(x, made_a))
    ours = lax.optimization_barrier((above, *ours))[1:]
    ours = [o.reshape(2, piece, radial, width) for o in ours]
    passed = [lax.dynamic_index_in_dim(o, 1 - core, 0) for o in ours]
    theirs = swap(jnp.concatenate(passed, 0), 1)
    where = jnp.stack([row, core]).astype(jnp.int32)
    *made_b, passed = radial_apart(where, after(matrix, above, from_ahead, from_below), ours, theirs)
    passed = swap(passed, 1)
    joint = [jnp.concatenate([made_b[d], passed[d]], 0) for d in range(chips)]
    back_b = [joint[0]] + [swap(joint[d], 2 * d) for d in range(1, chips)]

    upper = from_ahead.reshape(rows, width)
    lower = from_below.reshape(rows, width)
    out = middle_terms(
        basis_sizes, coupling, where, below, above, x, lower, upper,
        back_a.reshape(joined * radial, width), joint[0].reshape(2 * piece * radial, width),
        inertia_local, factor,
    )
    out = out.reshape(columns * radial, width)
    back_b = [b.reshape(2 * piece * radial, width) for b in back_b]
    out = add_apart(
        basis, joined // (2 * piece), where, basis_sizes, out, back_b[1:], factor
    )
    return out.reshape(packet.shape)


def solution(mesh):
    in_specs = (
        P("ka", None, "row", None),
        P("ka", None, "row", None),
        P("ka"),
        P("ka", None),
        P(),
        P(),
        P("row"),
        P(),
        P(),
        P("ka", None, None),
        P(None, "row", None),
    )
    out_specs = P("ka", None, "row", None)
    return jax.shard_map(shards, mesh=mesh, in_specs=in_specs, out_specs=out_specs, check_vma=False)
```

```python
import functools

import jax
import jax.numpy as jnp
from jax import lax
from jax.experimental import pallas as pl
from jax.experimental.pallas import tpu as pltpu
from jax.sharding import PartitionSpec as P

F32 = jnp.float32
BF16 = jnp.bfloat16
MIB = 1 << 20
BRIEF = pl.CostEstimate(flops=1, bytes_accessed=1, transcendentals=0)


def from_behind(x, axis, by):
    peers = lax.axis_size(axis)
    pairs = [(i, i + by) for i in range(peers) if 0 <= i + by < peers]
    return lax.ppermute(x, axis, pairs)


def exchange(x):
    return lax.all_to_all(x, "row", split_axis=0, concat_axis=0, tiled=True)


def halves(x):
    high = x.astype(BF16)
    return high, (x - high.astype(F32)).astype(BF16)


def halves_outside(x):
    high = lax.reduce_precision(x, 8, 7)
    return high.astype(BF16), (x - high).astype(BF16)


def leading_kernel(x_ref, out_ref, held, come, go):
    parts, size = held.shape[:2]
    into = [
        pltpu.make_async_copy(x_ref.at[pl.ds(i * size, size)], held.at[i], come.at[i])
        for i in range(parts)
    ]
    onward = [
        pltpu.make_async_copy(held.at[i], out_ref.at[pl.ds(i * size, size)], go.at[i])
        for i in range(parts)
    ]
    for copy in into:
        copy.start()
    for i in range(parts):
        into[i].wait()
        onward[i].start()
    for copy in onward:
        copy.wait()


def leading(x, count):
    parts = 4
    return pl.pallas_call(
        leading_kernel,
        in_specs=[pl.BlockSpec(memory_space=pl.ANY)],
        out_specs=pl.BlockSpec(memory_space=pl.ANY),
        out_shape=jax.ShapeDtypeStruct((count, *x.shape[1:]), F32),
        scratch_shapes=[
            pltpu.VMEM((parts, count // parts, *x.shape[1:]), F32),
            pltpu.SemaphoreType.DMA((parts,)),
            pltpu.SemaphoreType.DMA((parts,)),
        ],
        cost_estimate=BRIEF,
        name="leading",
    )(x)


def local_kernel(
    block, sizes, centrifugal, x_ref, previous_ref, potential_ref, legendre_ref, stretch_ref,
    inertia_ref, factor_ref, out_ref, acc, ahead, back,
):
    live = sizes[block]
    angles, basis = legendre_ref.shape[1:]
    radial = inertia_ref.shape[0]
    rows = basis * radial
    high, low = halves(legendre_ref[0])
    ahead[:, :basis] = high
    ahead[:, basis : 2 * basis] = high
    ahead[:, 2 * basis :] = low
    high, low = halves(legendre_ref[0].T)
    back[:, :angles] = high
    back[:, angles : 2 * angles] = high
    back[:, 2 * angles :] = low

    piece = rows // 8

    @pl.loop(0, 8)
    def _(i):
        at = pl.ds(pl.multiple_of(i * piece, piece), piece)
        high, low = halves(x_ref[0, at, :])
        both = jnp.dot(
            jnp.concatenate([high, low], 1), stretch_ref[...], preferred_element_type=F32
        )
        acc[at, :] = both[:, :128] + both[:, 128:]

    mask = lax.broadcasted_iota(jnp.int32, (basis, 256), 0) < live

    @pl.loop(0, radial // 2)
    def _(i):
        r = 2 * i
        here = [pl.ds(r + k, basis, stride=radial) for k in range(2)]
        there = [pl.ds(r + k, angles, stride=radial) for k in range(2)]
        m = jnp.concatenate([x_ref[0, at, :] for at in here], 1)
        m = jnp.where(mask, m, 0.0)
        high, low = halves(m)
        grid = jnp.dot(
            ahead[...], jnp.concatenate([high, low, high], 0), preferred_element_type=F32
        )
        grid = grid * jnp.concatenate([potential_ref[at, :] for at in there], 1)
        high, low = halves(grid)
        term = jnp.dot(
            back[...], jnp.concatenate([high, low, high], 0), preferred_element_type=F32
        )
        for k in range(2):
            acc[here[k], :] += term[:, 128 * k : 128 * (k + 1)]

    inertia = inertia_ref[...]
    factor = factor_ref[...]

    @pl.loop(0, basis // 8)
    def _(i):
        for k in range(8):
            j = i * 8 + k
            at = pl.ds(pl.multiple_of(j * radial, radial), radial)
            value = acc[at, :] + (centrifugal[block, j] * inertia) * x_ref[0, at, :]
            value = factor * (2.0 * value - factor * previous_ref[0, at, :])
            out_ref[0, at, :] = jnp.where(j < live, value, 0.0)


def local_terms(block, sizes, centrifugal, x, previous, potential, legendre, stretch, inertia, factor):
    angles, basis = legendre.shape[1:]
    rows = x.shape[1]
    whole = pl.BlockSpec((1, rows, 128), lambda k: (block, 0, 0))
    smem = pl.BlockSpec(memory_space=pltpu.SMEM)
    once = lambda shape: pl.BlockSpec(shape, lambda k: (0,) * len(shape))
    return pl.pallas_call(
        functools.partial(local_kernel, block),
        grid=(1,),
        in_specs=[
            smem, smem, whole, whole, once(potential.shape),
            pl.BlockSpec((1, angles, basis), lambda k: (block, 0, 0)),
            once(stretch.shape), once(inertia.shape), once(factor.shape),
        ],
        out_specs=once((1, rows, 128)),
        out_shape=jax.ShapeDtypeStruct((1, rows, 128), F32),
        scratch_shapes=[
            pltpu.VMEM((rows, 128), F32),
            pltpu.VMEM((angles, 3 * basis), BF16),
            pltpu.VMEM((basis, 3 * angles), BF16),
        ],
        compiler_params=pltpu.CompilerParams(vmem_limit_bytes=60 * MIB),
        cost_estimate=BRIEF,
        name="local_terms",
    )(sizes, centrifugal, x, previous, potential, legendre, stretch, inertia, factor)


def pair_product(matrix, pair):
    m = jnp.concatenate(pair, 1)
    high, low = halves(m)
    both = jnp.dot(matrix, jnp.concatenate([high, low], 0), preferred_element_type=F32)
    half = both.shape[0] // 2
    total = both[:half] + both[half:]
    return total[:, :128], total[:, 128:]


def radial_kernel(matrix_ref, x_ref, out_ref):
    peers, columns, rows, width = x_ref.shape
    for c in range(0, columns, 2):
        pair = [x_ref[:, c + k].reshape(peers * rows, width) for k in range(2)]
        for k, total in enumerate(pair_product(matrix_ref[...], pair)):
            out_ref[:, c + k] = total.reshape(peers, rows, width)


def radial_apply(matrix, received):
    peers, columns, rows, width = received.shape
    some = pl.BlockSpec((peers, 16, rows, width), lambda i: (0, i, 0, 0))
    return pl.pallas_call(
        radial_kernel,
        grid=(columns // 16,),
        in_specs=[pl.BlockSpec(matrix.shape, lambda i: (0, 0)), some],
        out_specs=some,
        out_shape=jax.ShapeDtypeStruct(received.shape, F32),
        compiler_params=pltpu.CompilerParams(vmem_limit_bytes=60 * MIB),
        cost_estimate=BRIEF,
        name="radial_apply",
    )(matrix, received)


def radial_apart_kernel(where_ref, matrix_ref, *refs):
    *ours, theirs, out_theirs, turned = refs
    chips = len(ours) // 2
    ours, outs = ours[:chips], ours[chips:]
    columns, rows, width = theirs.shape[1:]

    @pl.when(pl.program_id(0) == 0)
    def _():
        size = matrix_ref.shape[0]
        i = lax.broadcasted_iota(jnp.int32, (size, size), 0)
        j = lax.broadcasted_iota(jnp.int32, (size, size), 1)
        moved = jnp.where(j == (i ^ (where_ref[0] * rows)), 1.0, 0.0).astype(BF16)
        half = jnp.dot(moved, matrix_ref[...], preferred_element_type=F32).astype(BF16)
        turned[...] = jnp.dot(half, moved, preferred_element_type=F32).astype(BF16)

    for c in range(0, columns, 2):
        pair = []
        for k in range(2):
            pieces = []
            for d in range(chips):
                pieces += [ours[d][0, c + k], theirs[d, c + k]]
            pair.append(jnp.concatenate(pieces, 0))
        for k, total in enumerate(pair_product(turned[...], pair)):
            for d in range(chips):
                at = 2 * d * rows
                outs[d][c + k] = total[at : at + rows]
                out_theirs[d, c + k] = total[at + rows : at + 2 * rows]


def radial_apart(where, matrix, ours, theirs):
    chips = len(ours)
    columns, rows, width = theirs.shape[1:]
    mine = pl.BlockSpec((1, 8, rows, width), lambda i, where: (where[1], i, 0, 0))
    made = pl.BlockSpec((8, rows, width), lambda i, where: (i, 0, 0))
    all_chips = pl.BlockSpec((chips, 8, rows, width), lambda i, where: (0, i, 0, 0))

    def kernel(where_ref, matrix_ref, *refs):
        ins, theirs_ref = refs[:chips], refs[chips]
        outs, out_theirs, turned = refs[chips + 1 : 2 * chips + 1], refs[-2], refs[-1]
        radial_apart_kernel(where_ref, matrix_ref, *ins, *outs, theirs_ref, out_theirs, turned)

    return pl.pallas_call(
        kernel,
        grid_spec=pltpu.PrefetchScalarGridSpec(
            num_scalar_prefetch=1,
            grid=(columns // 8,),
            in_specs=[pl.BlockSpec(matrix.shape, lambda i, where: (0, 0))]
            + [mine] * chips + [all_chips],
            out_specs=[made] * chips + [all_chips],
            scratch_shapes=[pltpu.VMEM(matrix.shape, BF16)],
        ),
        out_shape=[jax.ShapeDtypeStruct(theirs.shape[1:], F32)] * chips
        + [jax.ShapeDtypeStruct(theirs.shape, F32)],
        cost_estimate=BRIEF,
        name="radial_apart",
    )(where, matrix, *ours, theirs)


def middle_kernel(
    sizes, coriolis, where, below_ref, above_ref, x_ref, lower_ref, upper_ref, first_ref, second_ref,
    own_ref, inertia_ref, factor_ref, out_ref
):
    step = pl.program_id(0)
    radial = inertia_ref.shape[0]
    count = x_ref.shape[1] // radial
    double = 2.0 * factor_ref[...]
    inertia = inertia_ref[...]
    below, above = sizes[0], sizes[1]

    def part(more):
        @pl.loop(0, count // 4)
        def _(i):
            for k in range(4):
                local = i * 4 + k
                j = step * count + local
                at = pl.ds(pl.multiple_of(local * radial, radial), radial)
                here = jnp.where(j < below, x_ref[0, at, :], 0.0)
                there = jnp.where(j < above, x_ref[1, at, :], 0.0)
                low = coriolis[1, j] * there + coriolis[0, j] * lower_ref[at, :]
                high = coriolis[2, j] * upper_ref[at, :] + coriolis[1, j] * here
                low = double * (inertia * low + first_ref[at, :])
                high = inertia * high
                if more:
                    high = high + second_ref[at, :]
                high = double * high
                out_ref[0, at, :] = below_ref[0, at, :] + jnp.where(j < below, low, 0.0)
                out_ref[1, at, :] = above_ref[0, at, :] + jnp.where(j < above, high, 0.0)

    pl.when(step < SECOND_PARTS)(lambda: part(True))
    pl.when(step >= SECOND_PARTS)(lambda: part(False))
    own = SECOND_PARTS + where[0] // 2 * 2

    @pl.when((step == own) | (step == own + 1))
    def _():
        start = ((step - own) ^ where[1]) * count

        @pl.loop(0, count // 4)
        def _(i):
            for k in range(4):
                local = i * 4 + k
                at = pl.ds(pl.multiple_of(local * radial, radial), radial)
                of = pl.ds(pl.multiple_of((start + local) * radial, radial), radial)
                more = jnp.where(step * count + local < above, double * own_ref[of, :], 0.0)
                out_ref[1, at, :] += more


MIDDLE_PARTS = 12
SECOND_PARTS = 4


def middle_terms(
    sizes, coriolis, where, below, above, x, lower, upper, back, own, inertia, factor
):
    blocks, rows, width = x.shape
    size = rows // MIDDLE_PARTS
    assert back.shape[0] == rows + size * SECOND_PARTS and own.shape[0] == 2 * size
    smem = pl.BlockSpec(memory_space=pltpu.SMEM)
    pair = pl.BlockSpec((blocks, size, width), lambda i: (0, i, 0))
    single = pl.BlockSpec((1, size, width), lambda i: (0, i, 0))
    one = pl.BlockSpec((size, width), lambda i: (i, 0))
    second = pl.BlockSpec((size, width), lambda i: (MIDDLE_PARTS + jnp.minimum(i, SECOND_PARTS - 1), 0))
    small = pl.BlockSpec(inertia.shape, lambda i: (0, 0))
    return pl.pallas_call(
        middle_kernel,
        grid=(MIDDLE_PARTS,),
        in_specs=[
            smem, smem, smem, single, single, pair, one, one, one, second,
            pl.BlockSpec(own.shape, lambda i: (0, 0)), small, small,
        ],
        out_specs=pair,
        out_shape=jax.ShapeDtypeStruct(x.shape, F32),
        compiler_params=pltpu.CompilerParams(vmem_limit_bytes=60 * MIB),
        cost_estimate=BRIEF,
        name="middle_terms",
    )(sizes, coriolis, where, below, above, x, lower, upper, back, back, own, inertia, factor)


def add_apart_kernel(basis, lead, where, sizes, out_in, factor_ref, *refs):
    backs, (out_ref, held, sems, end_sems) = refs[:-4], refs[-4:]
    radial = factor_ref.shape[0]
    rows = held.shape[1]
    columns = rows // radial
    half = columns // 2
    double = 2.0 * factor_ref[...]
    places = [lead + (where[0] // 2 ^ (i + 1)) for i in range(len(backs))]
    windows = [out_ref.at[pl.ds(pl.multiple_of(p * rows, rows), rows), :] for p in places]
    reads = [
        pltpu.make_async_copy(w, held.at[i], sems.at[i]) for i, w in enumerate(windows)
    ]
    writes = [
        pltpu.make_async_copy(held.at[i], w, end_sems.at[i]) for i, w in enumerate(windows)
    ]
    for read in reads:
        read.start()
    for i in range(len(backs)):
        reads[i].wait()
        begin = places[i] * columns
        live = jnp.where(begin < basis, sizes[0], sizes[1] + basis) - begin
        for core in range(2):
            shift = (where[1] ^ core) - core

            @pl.loop(0, half // 8)
            def _(c):
                for k in range(8):
                    j = core * half + c * 8 + k
                    at = pl.ds(pl.multiple_of(j * radial, radial), radial)
                    of = pl.ds(pl.multiple_of((j + shift * half) * radial, radial), radial)
                    held[i, at, :] += jnp.where(j < live, double * backs[i][of, :], 0.0)
        writes[i].start()
    for write in writes:
        write.wait()


def add_apart(basis, lead, where, sizes, out, backs, factor):
    rows, width = backs[0].shape
    count = len(backs)
    smem = pl.BlockSpec(memory_space=pltpu.SMEM)
    whole = pl.BlockSpec(memory_space=pl.ANY)
    return pl.pallas_call(
        functools.partial(add_apart_kernel, basis, lead),
        in_specs=[smem, smem, whole] + [pl.BlockSpec(memory_space=pltpu.VMEM)] * (1 + count),
        out_specs=whole,
        out_shape=jax.ShapeDtypeStruct(out.shape, F32),
        input_output_aliases={2: 0},
        scratch_shapes=[
            pltpu.VMEM((count, rows, width), F32),
            pltpu.SemaphoreType.DMA((count,)),
            pltpu.SemaphoreType.DMA((count,)),
        ],
        compiler_params=pltpu.CompilerParams(vmem_limit_bytes=16 * MIB),
        cost_estimate=BRIEF,
        name="add_apart",
    )(where, sizes, out, factor, *backs)


def swap(x, by):
    peers = lax.axis_size("row")
    return lax.ppermute(x, "row", [(i, i ^ by) for i in range(peers)])


def after(x, *first):
    return lax.optimization_barrier((x, *first))[0]


def shards(
    packet, previous, basis_sizes, centrifugal, coriolis, inertia, damping,
    radial_kin, stretch_kin, legendre, potential,
):
    blocks, basis, radial, width = packet.shape
    peers = lax.axis_size("row")
    ka = lax.axis_index("ka")
    row = lax.axis_index("row")
    columns = blocks * basis
    rows = basis * radial
    joined = 2 * columns // 3
    piece = (columns - joined) // peers
    chips = peers // 2
    x_chip, core = row // 2, row % 2

    flat = packet.reshape(columns, radial, width)
    def part(x, d):
        return lax.dynamic_slice_in_dim(x, joined + (x_chip ^ d) * 2 * piece, 2 * piece, 0)

    sent_a = leading(flat, joined)
    got_a = exchange(sent_a)
    source = after(flat, sent_a)
    order = tuple(reversed(range(chips)))
    sent = {d: part(source, d) for d in order}
    ours = {d: swap(sent[d], 2 * d) if d else sent[d] for d in order}
    ours = [ours[d] for d in range(chips)]

    live_mask = (lax.broadcasted_iota(jnp.int32, (blocks, basis), 1) < basis_sizes[:, None]).astype(F32)
    source = after(packet, *sent.values())
    upper = source[:1] * live_mask[:1, :, None, None]
    lower = source[1:] * live_mask[1:, :, None, None]
    from_ahead = from_behind(upper, "ka", -1)
    from_below = from_behind(lower, "ka", 1)

    inertia_local = lax.dynamic_slice_in_dim(inertia, row * radial, radial, 0)
    factor = jnp.broadcast_to(damping[:, None], (radial, width))
    t_high, t_low = halves_outside(radial_kin)
    t_high, t_low = [jnp.concatenate([t, t], 1) for t in (t_high, t_low)]
    matrix = jnp.concatenate([t_high, t_low], 0)
    s_high, s_low = halves_outside(stretch_kin.T)
    stretch = jnp.concatenate([jnp.concatenate([s_high, s_low], 1)] * 2, 0)
    start = jnp.maximum(ka * blocks - 1, 0)
    coupling = jnp.concatenate(
        [lax.dynamic_slice_in_dim(coriolis, start, 1, 0),
         lax.dynamic_slice_in_dim(coriolis, ka * blocks, blocks, 0)], 0
    )

    x = packet.reshape(blocks, rows, width)
    before = previous.reshape(blocks, rows, width)
    grid = potential.reshape(potential.shape[0] * radial, width)

    def local(block, x):
        return local_terms(
            block, basis_sizes, centrifugal, x, before, grid, legendre, stretch, inertia_local, factor
        )

    below = local(0, after(x, upper, lower))
    made_a = radial_apply(after(matrix, below), got_a.reshape(peers, joined // peers, radial, width))
    back_a = exchange(made_a.reshape(joined, radial, width))
    above = local(1, after(x, made_a))
    ours = lax.optimization_barrier((above, *ours))[1:]
    ours = [o.reshape(2, piece, radial, width) for o in ours]
    passed = [lax.dynamic_index_in_dim(o, 1 - core, 0) for o in ours]
    theirs = swap(jnp.concatenate(passed, 0), 1)
    where = jnp.stack([row, core]).astype(jnp.int32)
    *made_b, passed = radial_apart(where, after(matrix, above, from_ahead, from_below), ours, theirs)
    passed = swap(passed, 1)
    joint = [jnp.concatenate([made_b[d], passed[d]], 0) for d in range(chips)]
    back_b = [joint[0]] + [swap(joint[d], 2 * d) for d in range(1, chips)]

    upper = from_ahead.reshape(rows, width)
    lower = from_below.reshape(rows, width)
    out = middle_terms(
        basis_sizes, coupling, where, below, above, x, lower, upper,
        back_a.reshape(joined * radial, width), joint[0].reshape(2 * piece * radial, width),
        inertia_local, factor,
    )
    out = out.reshape(columns * radial, width)
    back_b = [b.reshape(2 * piece * radial, width) for b in back_b]
    out = add_apart(
        basis, joined // (2 * piece), where, basis_sizes, out, back_b[1:], factor
    )
    return out.reshape(packet.shape)


def solution(mesh):
    in_specs = (
        P("ka", None, "row", None),
        P("ka", None, "row", None),
        P("ka"),
        P("ka", None),
        P(),
        P(),
        P("row"),
        P(),
        P(),
        P("ka", None, None),
        P(None, "row", None),
    )
    out_specs = P("ka", None, "row", None)
    return jax.shard_map(shards, mesh=mesh, in_specs=in_specs, out_specs=out_specs, check_vma=False)
```

```python
import functools

import jax
import jax.numpy as jnp
from jax import lax
from jax.experimental import pallas as pl
from jax.experimental.pallas import tpu as pltpu
from jax.sharding import PartitionSpec as P

F32 = jnp.float32
BF16 = jnp.bfloat16
MIB = 1 << 20
BRIEF = pl.CostEstimate(flops=1, bytes_accessed=1, transcendentals=0)


def from_behind(x, axis, by):
    peers = lax.axis_size(axis)
    pairs = [(i, i + by) for i in range(peers) if 0 <= i + by < peers]
    return lax.ppermute(x, axis, pairs)


def exchange(x):
    return lax.all_to_all(x, "row", split_axis=0, concat_axis=0, tiled=True)


def halves(x):
    high = x.astype(BF16)
    return high, (x - high.astype(F32)).astype(BF16)


def halves_outside(x):
    high = lax.reduce_precision(x, 8, 7)
    return high.astype(BF16), (x - high).astype(BF16)


def leading_kernel(x_ref, out_ref, held, come, go):
    parts, size = held.shape[:2]
    into = [
        pltpu.make_async_copy(x_ref.at[pl.ds(i * size, size)], held.at[i], come.at[i])
        for i in range(parts)
    ]
    onward = [
        pltpu.make_async_copy(held.at[i], out_ref.at[pl.ds(i * size, size)], go.at[i])
        for i in range(parts)
    ]
    for copy in into:
        copy.start()
    for i in range(parts):
        into[i].wait()
        onward[i].start()
    for copy in onward:
        copy.wait()


def leading(x, count):
    parts = 4
    return pl.pallas_call(
        leading_kernel,
        in_specs=[pl.BlockSpec(memory_space=pl.ANY)],
        out_specs=pl.BlockSpec(memory_space=pl.ANY),
        out_shape=jax.ShapeDtypeStruct((count, *x.shape[1:]), F32),
        scratch_shapes=[
            pltpu.VMEM((parts, count // parts, *x.shape[1:]), F32),
            pltpu.SemaphoreType.DMA((parts,)),
            pltpu.SemaphoreType.DMA((parts,)),
        ],
        cost_estimate=BRIEF,
        name="leading",
    )(x)


def local_kernel(
    block, sizes, centrifugal, x_ref, previous_ref, potential_ref, legendre_ref, stretch_ref,
    inertia_ref, factor_ref, out_ref, acc, ahead, back,
):
    live = sizes[block]
    angles, basis = legendre_ref.shape[1:]
    radial = inertia_ref.shape[0]
    rows = basis * radial
    high, low = halves(legendre_ref[0])
    ahead[:, :basis] = high
    ahead[:, basis : 2 * basis] = high
    ahead[:, 2 * basis :] = low
    high, low = halves(legendre_ref[0].T)
    back[:, :angles] = high
    back[:, angles : 2 * angles] = high
    back[:, 2 * angles :] = low

    piece = rows // 8

    @pl.loop(0, 8)
    def _(i):
        at = pl.ds(pl.multiple_of(i * piece, piece), piece)
        high, low = halves(x_ref[0, at, :])
        both = jnp.dot(
            jnp.concatenate([high, low], 1), stretch_ref[...], preferred_element_type=F32
        )
        acc[at, :] = both[:, :128] + both[:, 128:]

    mask = lax.broadcasted_iota(jnp.int32, (basis, 256), 0) < live

    @pl.loop(0, radial // 2)
    def _(i):
        r = 2 * i
        here = [pl.ds(r + k, basis, stride=radial) for k in range(2)]
        there = [pl.ds(r + k, angles, stride=radial) for k in range(2)]
        m = jnp.concatenate([x_ref[0, at, :] for at in here], 1)
        m = jnp.where(mask, m, 0.0)
        high, low = halves(m)
        grid = jnp.dot(
            ahead[...], jnp.concatenate([high, low, high], 0), preferred_element_type=F32
        )
        grid = grid * jnp.concatenate([potential_ref[at, :] for at in there], 1)
        high, low = halves(grid)
        term = jnp.dot(
            back[...], jnp.concatenate([high, low, high], 0), preferred_element_type=F32
        )
        for k in range(2):
            acc[here[k], :] += term[:, 128 * k : 128 * (k + 1)]

    inertia = inertia_ref[...]
    factor = factor_ref[...]

    @pl.loop(0, basis // 8)
    def _(i):
        for k in range(8):
            j = i * 8 + k
            at = pl.ds(pl.multiple_of(j * radial, radial), radial)
            value = acc[at, :] + (centrifugal[block, j] * inertia) * x_ref[0, at, :]
            value = factor * (2.0 * value - factor * previous_ref[0, at, :])
            out_ref[0, at, :] = jnp.where(j < live, value, 0.0)


def local_terms(block, sizes, centrifugal, x, previous, potential, legendre, stretch, inertia, factor):
    angles, basis = legendre.shape[1:]
    rows = x.shape[1]
    whole = pl.BlockSpec((1, rows, 128), lambda k: (block, 0, 0))
    smem = pl.BlockSpec(memory_space=pltpu.SMEM)
    once = lambda shape: pl.BlockSpec(shape, lambda k: (0,) * len(shape))
    return pl.pallas_call(
        functools.partial(local_kernel, block),
        grid=(1,),
        in_specs=[
            smem, smem, whole, whole, once(potential.shape),
            pl.BlockSpec((1, angles, basis), lambda k: (block, 0, 0)),
            once(stretch.shape), once(inertia.shape), once(factor.shape),
        ],
        out_specs=once((1, rows, 128)),
        out_shape=jax.ShapeDtypeStruct((1, rows, 128), F32),
        scratch_shapes=[
            pltpu.VMEM((rows, 128), F32),
            pltpu.VMEM((angles, 3 * basis), BF16),
            pltpu.VMEM((basis, 3 * angles), BF16),
        ],
        compiler_params=pltpu.CompilerParams(vmem_limit_bytes=60 * MIB),
        cost_estimate=BRIEF,
        name="local_terms",
    )(sizes, centrifugal, x, previous, potential, legendre, stretch, inertia, factor)


def pair_product(matrix, pair):
    m = jnp.concatenate(pair, 1)
    high, low = halves(m)
    both = jnp.dot(matrix, jnp.concatenate([high, low], 0), preferred_element_type=F32)
    half = both.shape[0] // 2
    total = both[:half] + both[half:]
    return total[:, :128], total[:, 128:]


def radial_kernel(matrix_ref, x_ref, out_ref):
    peers, columns, rows, width = x_ref.shape
    for c in range(0, columns, 2):
        pair = [x_ref[:, c + k].reshape(peers * rows, width) for k in range(2)]
        for k, total in enumerate(pair_product(matrix_ref[...], pair)):
            out_ref[:, c + k] = total.reshape(peers, rows, width)


def radial_apply(matrix, received):
    peers, columns, rows, width = received.shape
    some = pl.BlockSpec((peers, 16, rows, width), lambda i: (0, i, 0, 0))
    return pl.pallas_call(
        radial_kernel,
        grid=(columns // 16,),
        in_specs=[pl.BlockSpec(matrix.shape, lambda i: (0, 0)), some],
        out_specs=some,
        out_shape=jax.ShapeDtypeStruct(received.shape, F32),
        compiler_params=pltpu.CompilerParams(vmem_limit_bytes=60 * MIB),
        cost_estimate=BRIEF,
        name="radial_apply",
    )(matrix, received)


def radial_apart_kernel(where_ref, matrix_ref, *refs):
    *ours, theirs, out_theirs, turned = refs
    chips = len(ours) // 2
    ours, outs = ours[:chips], ours[chips:]
    columns, rows, width = theirs.shape[1:]

    @pl.when(pl.program_id(0) == 0)
    def _():
        size = matrix_ref.shape[0]
        i = lax.broadcasted_iota(jnp.int32, (size, size), 0)
        j = lax.broadcasted_iota(jnp.int32, (size, size), 1)
        moved = jnp.where(j == (i ^ (where_ref[0] * rows)), 1.0, 0.0).astype(BF16)
        half = jnp.dot(moved, matrix_ref[...], preferred_element_type=F32).astype(BF16)
        turned[...] = jnp.dot(half, moved, preferred_element_type=F32).astype(BF16)

    for c in range(0, columns, 2):
        pair = []
        for k in range(2):
            pieces = []
            for d in range(chips):
                pieces += [ours[d][0, c + k], theirs[d, c + k]]
            pair.append(jnp.concatenate(pieces, 0))
        for k, total in enumerate(pair_product(turned[...], pair)):
            for d in range(chips):
                at = 2 * d * rows
                outs[d][c + k] = total[at : at + rows]
                out_theirs[d, c + k] = total[at + rows : at + 2 * rows]


def radial_apart(where, matrix, ours, theirs):
    chips = len(ours)
    columns, rows, width = theirs.shape[1:]
    mine = pl.BlockSpec((1, 8, rows, width), lambda i, where: (where[1], i, 0, 0))
    made = pl.BlockSpec((8, rows, width), lambda i, where: (i, 0, 0))
    all_chips = pl.BlockSpec((chips, 8, rows, width), lambda i, where: (0, i, 0, 0))

    def kernel(where_ref, matrix_ref, *refs):
        ins, theirs_ref = refs[:chips], refs[chips]
        outs, out_theirs, turned = refs[chips + 1 : 2 * chips + 1], refs[-2], refs[-1]
        radial_apart_kernel(where_ref, matrix_ref, *ins, *outs, theirs_ref, out_theirs, turned)

    return pl.pallas_call(
        kernel,
        grid_spec=pltpu.PrefetchScalarGridSpec(
            num_scalar_prefetch=1,
            grid=(columns // 8,),
            in_specs=[pl.BlockSpec(matrix.shape, lambda i, where: (0, 0))]
            + [mine] * chips + [all_chips],
            out_specs=[made] * chips + [all_chips],
            scratch_shapes=[pltpu.VMEM(matrix.shape, BF16)],
        ),
        out_shape=[jax.ShapeDtypeStruct(theirs.shape[1:], F32)] * chips
        + [jax.ShapeDtypeStruct(theirs.shape, F32)],
        cost_estimate=BRIEF,
        name="radial_apart",
    )(where, matrix, *ours, theirs)


def middle_kernel(
    sizes, coriolis, where, below_ref, above_ref, x_ref, lower_ref, upper_ref, first_ref, second_ref,
    own_ref, inertia_ref, factor_ref, out_ref
):
    step = pl.program_id(0)
    radial = inertia_ref.shape[0]
    count = x_ref.shape[1] // radial
    double = 2.0 * factor_ref[...]
    inertia = inertia_ref[...]
    below, above = sizes[0], sizes[1]

    def part(more):
        @pl.loop(0, count // 4)
        def _(i):
            for k in range(4):
                local = i * 4 + k
                j = step * count + local
                at = pl.ds(pl.multiple_of(local * radial, radial), radial)
                here = jnp.where(j < below, x_ref[0, at, :], 0.0)
                there = jnp.where(j < above, x_ref[1, at, :], 0.0)
                low = coriolis[1, j] * there + coriolis[0, j] * lower_ref[at, :]
                high = coriolis[2, j] * upper_ref[at, :] + coriolis[1, j] * here
                low = double * (inertia * low + first_ref[at, :])
                high = inertia * high
                if more:
                    high = high + second_ref[at, :]
                high = double * high
                out_ref[0, at, :] = below_ref[0, at, :] + jnp.where(j < below, low, 0.0)
                out_ref[1, at, :] = above_ref[0, at, :] + jnp.where(j < above, high, 0.0)

    pl.when(step < SECOND_PARTS)(lambda: part(True))
    pl.when(step >= SECOND_PARTS)(lambda: part(False))
    own = SECOND_PARTS + where[0] // 2 * 2

    @pl.when((step == own) | (step == own + 1))
    def _():
        start = ((step - own) ^ where[1]) * count

        @pl.loop(0, count // 4)
        def _(i):
            for k in range(4):
                local = i * 4 + k
                at = pl.ds(pl.multiple_of(local * radial, radial), radial)
                of = pl.ds(pl.multiple_of((start + local) * radial, radial), radial)
                more = jnp.where(step * count + local < above, double * own_ref[of, :], 0.0)
                out_ref[1, at, :] += more


MIDDLE_PARTS = 12
SECOND_PARTS = 4


def middle_terms(
    sizes, coriolis, where, below, above, x, lower, upper, back, own, inertia, factor
):
    blocks, rows, width = x.shape
    size = rows // MIDDLE_PARTS
    assert back.shape[0] == rows + size * SECOND_PARTS and own.shape[0] == 2 * size
    smem = pl.BlockSpec(memory_space=pltpu.SMEM)
    pair = pl.BlockSpec((blocks, size, width), lambda i: (0, i, 0))
    single = pl.BlockSpec((1, size, width), lambda i: (0, i, 0))
    one = pl.BlockSpec((size, width), lambda i: (i, 0))
    second = pl.BlockSpec((size, width), lambda i: (MIDDLE_PARTS + jnp.minimum(i, SECOND_PARTS - 1), 0))
    small = pl.BlockSpec(inertia.shape, lambda i: (0, 0))
    return pl.pallas_call(
        middle_kernel,
        grid=(MIDDLE_PARTS,),
        in_specs=[
            smem, smem, smem, single, single, pair, one, one, one, second,
            pl.BlockSpec(own.shape, lambda i: (0, 0)), small, small,
        ],
        out_specs=pair,
        out_shape=jax.ShapeDtypeStruct(x.shape, F32),
        compiler_params=pltpu.CompilerParams(vmem_limit_bytes=60 * MIB),
        cost_estimate=BRIEF,
        name="middle_terms",
    )(sizes, coriolis, where, below, above, x, lower, upper, back, back, own, inertia, factor)


def add_apart_kernel(basis, lead, where, sizes, out_in, factor_ref, *refs):
    backs, (out_ref, held, sems, end_sems) = refs[:-4], refs[-4:]
    radial = factor_ref.shape[0]
    rows = held.shape[1]
    columns = rows // radial
    half = columns // 2
    double = 2.0 * factor_ref[...]
    places = [lead + (where[0] // 2 ^ (i + 1)) for i in range(len(backs))]
    reads, writes = [], []
    part = rows // 2
    for i, p in enumerate(places):
        for core in range(2):
            start = pl.multiple_of((2 * p + core) * part, part)
            window = out_ref.at[pl.ds(start, part), :]
            kept = held.at[i, pl.ds(core * part, part), :]
            n = 2 * i + core
            reads.append(pltpu.make_async_copy(window, kept, sems.at[n]))
            writes.append(pltpu.make_async_copy(kept, window, end_sems.at[n]))
    for read in reads:
        read.start()
    for i in range(len(backs)):
        begin = places[i] * columns
        live = jnp.where(begin < basis, sizes[0], sizes[1] + basis) - begin
        for core in range(2):
            shift = (where[1] ^ core) - core
            reads[2 * i + core].wait()

            @pl.loop(0, half // 8)
            def _(c):
                for k in range(8):
                    j = core * half + c * 8 + k
                    at = pl.ds(pl.multiple_of(j * radial, radial), radial)
                    of = pl.ds(pl.multiple_of((j + shift * half) * radial, radial), radial)
                    held[i, at, :] += jnp.where(j < live, double * backs[i][of, :], 0.0)

            writes[2 * i + core].start()
    for write in writes:
        write.wait()


def add_apart(basis, lead, where, sizes, out, backs, factor):
    rows, width = backs[0].shape
    count = len(backs)
    smem = pl.BlockSpec(memory_space=pltpu.SMEM)
    whole = pl.BlockSpec(memory_space=pl.ANY)
    return pl.pallas_call(
        functools.partial(add_apart_kernel, basis, lead),
        in_specs=[smem, smem, whole] + [pl.BlockSpec(memory_space=pltpu.VMEM)] * (1 + count),
        out_specs=whole,
        out_shape=jax.ShapeDtypeStruct(out.shape, F32),
        input_output_aliases={2: 0},
        scratch_shapes=[
            pltpu.VMEM((count, rows, width), F32),
            pltpu.SemaphoreType.DMA((2 * count,)),
            pltpu.SemaphoreType.DMA((2 * count,)),
        ],
        compiler_params=pltpu.CompilerParams(vmem_limit_bytes=16 * MIB),
        cost_estimate=BRIEF,
        name="add_apart",
    )(where, sizes, out, factor, *backs)


def swap(x, by):
    peers = lax.axis_size("row")
    return lax.ppermute(x, "row", [(i, i ^ by) for i in range(peers)])


def after(x, *first):
    return lax.optimization_barrier((x, *first))[0]


def shards(
    packet, previous, basis_sizes, centrifugal, coriolis, inertia, damping,
    radial_kin, stretch_kin, legendre, potential,
):
    blocks, basis, radial, width = packet.shape
    peers = lax.axis_size("row")
    ka = lax.axis_index("ka")
    row = lax.axis_index("row")
    columns = blocks * basis
    rows = basis * radial
    joined = 2 * columns // 3
    piece = (columns - joined) // peers
    chips = peers // 2
    x_chip, core = row // 2, row % 2

    flat = packet.reshape(columns, radial, width)
    def part(x, d):
        return lax.dynamic_slice_in_dim(x, joined + (x_chip ^ d) * 2 * piece, 2 * piece, 0)

    sent_a = leading(flat, joined)
    got_a = exchange(sent_a)
    source = after(flat, sent_a)
    order = tuple(reversed(range(chips)))
    sent = {d: part(source, d) for d in order}
    ours = {d: swap(sent[d], 2 * d) if d else sent[d] for d in order}
    ours = [ours[d] for d in range(chips)]

    live_mask = (lax.broadcasted_iota(jnp.int32, (blocks, basis), 1) < basis_sizes[:, None]).astype(F32)
    source = after(packet, *sent.values())
    upper = source[:1] * live_mask[:1, :, None, None]
    lower = source[1:] * live_mask[1:, :, None, None]
    from_ahead = from_behind(upper, "ka", -1)
    from_below = from_behind(lower, "ka", 1)

    inertia_local = lax.dynamic_slice_in_dim(inertia, row * radial, radial, 0)
    factor = jnp.broadcast_to(damping[:, None], (radial, width))
    t_high, t_low = halves_outside(radial_kin)
    t_high, t_low = [jnp.concatenate([t, t], 1) for t in (t_high, t_low)]
    matrix = jnp.concatenate([t_high, t_low], 0)
    s_high, s_low = halves_outside(stretch_kin.T)
    stretch = jnp.concatenate([jnp.concatenate([s_high, s_low], 1)] * 2, 0)
    start = jnp.maximum(ka * blocks - 1, 0)
    coupling = jnp.concatenate(
        [lax.dynamic_slice_in_dim(coriolis, start, 1, 0),
         lax.dynamic_slice_in_dim(coriolis, ka * blocks, blocks, 0)], 0
    )

    x = packet.reshape(blocks, rows, width)
    before = previous.reshape(blocks, rows, width)
    grid = potential.reshape(potential.shape[0] * radial, width)

    def local(block, x):
        return local_terms(
            block, basis_sizes, centrifugal, x, before, grid, legendre, stretch, inertia_local, factor
        )

    below = local(0, after(x, upper, lower))
    made_a = radial_apply(after(matrix, below), got_a.reshape(peers, joined // peers, radial, width))
    back_a = exchange(made_a.reshape(joined, radial, width))
    above = local(1, after(x, made_a))
    ours = lax.optimization_barrier((above, *ours))[1:]
    ours = [o.reshape(2, piece, radial, width) for o in ours]
    passed = [lax.dynamic_index_in_dim(o, 1 - core, 0) for o in ours]
    theirs = swap(jnp.concatenate(passed, 0), 1)
    where = jnp.stack([row, core]).astype(jnp.int32)
    *made_b, passed = radial_apart(where, after(matrix, above, from_ahead, from_below), ours, theirs)
    passed = swap(passed, 1)
    joint = [jnp.concatenate([made_b[d], passed[d]], 0) for d in range(chips)]
    joint = [j if d in (0, 2) else after(j, joint[2]) for d, j in enumerate(joint)]
    back_b = [joint[0]] + [swap(joint[d], 2 * d) for d in range(1, chips)]

    upper = from_ahead.reshape(rows, width)
    lower = from_below.reshape(rows, width)
    out = middle_terms(
        basis_sizes, coupling, where, below, above, x, lower, upper,
        back_a.reshape(joined * radial, width), joint[0].reshape(2 * piece * radial, width),
        inertia_local, factor,
    )
    out = out.reshape(columns * radial, width)
    back_b = [b.reshape(2 * piece * radial, width) for b in back_b]
    out = add_apart(
        basis, joined // (2 * piece), where, basis_sizes, out, back_b[1:], factor
    )
    return out.reshape(packet.shape)


def solution(mesh):
    in_specs = (
        P("ka", None, "row", None),
        P("ka", None, "row", None),
        P("ka"),
        P("ka", None),
        P(),
        P(),
        P("row"),
        P(),
        P(),
        P("ka", None, None),
        P(None, "row", None),
    )
    out_specs = P("ka", None, "row", None)
    return jax.shard_map(shards, mesh=mesh, in_specs=in_specs, out_specs=out_specs, check_vma=False)
```
